32 devices in a mesh: groups: 2 (over y), wide: 4 (over z), narrow: 4 (over x, core).
Axes of the slice: x: 2, y: 2, z: 4, core: 2. Of those that a mesh axis runs over, the one named last changes fastest.
Arguments:
- generator: int32 [8192], P('narrow'), may hold values from 1 to 511
- lattice_shift: int32 [16384], P(('groups', 'narrow')), parts along dimension 0, may hold values from 0 to 1023
- loadings: bfloat16 [512, 4, 64, 128], P(('groups', 'wide')), parts along dimension 0, may hold values from -0.375 to 0.375
- load_pattern: int32 [512, 4], P(('groups', 'wide')), parts along dimension 0, may hold values from 0 to 127
- threshold: float32 [65536], P(('groups', 'wide')), parts along dimension 0, may hold values from -2.5 to -0.5
- exposure: float32 [65536], P(('groups', 'wide')), parts along dimension 0, may hold values from 0.1 to 2
- segment_map: int32 [65536], P(('groups', 'wide')), parts along dimension 0, may hold values from 0 to 4095, as said below
- net_tiles: bfloat16 [64, 8, 128, 128], P(('groups', 'wide')), parts along dimension 0, may hold values from -0.1875 to 0.1875
- net_pattern: int32 [64, 8], P(('groups', 'wide')), parts along dimension 0, may hold values from 0 to 7
Outputs:
- net_loss: float32 [512, 8192], P('narrow', ('groups', 'wide')), parts along dimension 1
- moments: float32 [2, 8192], P(None, ('groups', 'wide')), parts along dimension 1
The draws below stay inside these ranges and needn't reach their ends.
There are 2 independent parts, one for each index of `groups`. The reference program is written for one: setup_inputs(seed, part) draws one part's arguments, and reference() takes and returns one part's arrays. A program takes and returns all parts, laid end to end along the dimension named above; an argument that names none is the same for every part. Nothing has to cross between parts.
Inputs may be any that keep to these rules, and one draw needn't show every extreme that they name: `segment_map`: in each aligned block of 8192 obligors at most 3072 map to the same group of 1024 consecutive segments; one group receives exactly 3072 obligors from every block.
All inputs are finite; a program needn't handle non-finite values.
Results may differ from the reference program's by a relative error of at most 0.0036.
Values may be sent and summed in bfloat16 or wider, within the bound.
No kernel may reach another device: no remote copies, remote signals or barrier semaphores. Data moves between devices by JAX's collectives and lax.ppermute only.
A program may use at most 64 MiB of HBM per device.

```python
import math
import jax
import jax.numpy as jnp
from jax import lax

F = 8192
P_SIZE = 512
K = 4
KS = 8
O_DEV = 8192
SEG_DEV = 1024
O_TOTAL = 32768
SEGMENTS = 4096
CAP = 3072
N_WIDE = 4


def draw_segment_map(key, part):
    blocks = O_TOTAL // O_DEV
    slots = blocks * CAP
    keys = jax.random.split(key, 5)
    full_owner = jax.random.randint(keys[0], (), 0, blocks)
    leaning = jax.random.randint(keys[1], (blocks,), 0, 3)
    slot_owner = jnp.arange(slots, dtype=jnp.int32) // CAP
    scores = jax.random.randint(keys[2], (blocks, slots), 0, 65536)
    scores = jnp.right_shift(scores, leaning[slot_owner][None, :])
    scores = jnp.where(slot_owner[None, :] == full_owner, -1, scores)
    chosen = jnp.argsort(scores, axis=1, stable=True)[:, :O_DEV]
    owners = chosen // CAP
    row_keys = jax.random.split(keys[3], blocks)
    owners = jax.vmap(lambda row_key, row: jax.random.permutation(row_key, row))(row_keys, owners)
    local_seg = jax.random.randint(keys[4], (blocks, O_DEV), 0, SEG_DEV)
    return (owners * SEG_DEV + local_seg).reshape(-1).astype(jnp.int32)


def touch_ends(drawn, rng, smallest, high):
    longest = drawn.shape.index(max(drawn.shape))
    spots = []
    for shift in (0, 1):
        where = [jax.random.randint(jax.random.fold_in(rng, axis), (), 0, length) for axis, length in enumerate(drawn.shape)]
        where[longest] = (where[longest] + shift) % drawn.shape[longest]
        spots.append(tuple(where))
    return drawn.at[spots[0]].set(smallest).at[spots[1]].set(high)


def levels(key, dims, cuts, smallest, top_value):
    gain = 1.0
    for dim, blocks in cuts:
        steps = jax.random.uniform(jax.random.fold_in(jax.random.fold_in(key, 6), dim), (blocks,), jnp.float32, smallest / len(cuts), top_value / len(cuts))
        gain = gain * jnp.repeat(jnp.exp(steps), dims[dim] // blocks).reshape((-1,) + (1,) * (len(dims) - 1 - dim))
    return gain


def scatter_about(rng, shape, deviation, limit, cuts=(), kind=jnp.bfloat16):
    drawn = jax.random.normal(rng, shape, jnp.float32) * deviation
    if len(cuts) > 0:
        drawn = levels(rng, shape, cuts, -0.22, 0.18) * drawn
    return jnp.clip(drawn, min=-limit, max=limit).astype(kind)


def setup_inputs(seed: int = 0, part: int = 0) -> dict:
    arg_keys = jax.random.split(jax.random.key(seed), 10)
    part_splits = jax.random.split(jax.random.fold_in(arg_keys[9], part), 10)
    return {
        "generator": touch_ends(jax.random.randint(arg_keys[0], (F,), 1, P_SIZE), jax.random.fold_in(arg_keys[0], 1), 1, P_SIZE - 1).astype(jnp.int32),
        "lattice_shift": touch_ends(jax.random.randint(part_splits[1], (F,), 0, 1024), jax.random.fold_in(part_splits[1], 1), 0, 1023).astype(jnp.int32),
        "loadings": scatter_about(part_splits[2], (O_TOTAL // 128, K, 64, 128), (K * 64) ** -0.5, 0.375, ((0, 4),)),
        "load_pattern": touch_ends(jax.random.randint(part_splits[3], (O_TOTAL // 128, K), 0, F // 64), jax.random.fold_in(part_splits[3], 1), 0, (F // 64) - 1).astype(jnp.int32),
        "threshold": jnp.clip(-2.5 + 2.0 * jax.random.uniform(part_splits[4], (O_TOTAL,), jnp.float32) ** levels(part_splits[4], (O_TOTAL,), ((0, 4),), -0.2, 0.2), -2.5, -0.5),
        "exposure": jnp.clip(jnp.exp(math.log(2.0) - 2.9957323 * jax.random.uniform(part_splits[5], (O_TOTAL,), jnp.float32) ** levels(part_splits[5], (O_TOTAL,), ((0, 4),), -0.2, 0.2)), 0.1, 2.0),
        "segment_map": draw_segment_map(jax.random.fold_in(jax.random.fold_in(arg_keys[9], part), 71), part),
        "net_tiles": scatter_about(part_splits[7], (SEGMENTS // 128, KS, 128, 128), (KS * 128) ** -0.5, 0.1875, ((0, 4),)),
        "net_pattern": touch_ends(jax.random.randint(part_splits[8], (SEGMENTS // 128, KS), 0, SEG_DEV // 128), jax.random.fold_in(part_splits[8], 1), 0, (SEG_DEV // 128) - 1).astype(jnp.int32),
    }


def normal_cdf(values):
    return 0.5 * lax.erfc(-values * 0.7071067811865476)


def normal_quantile(values):
    return 1.4142135623730951 * lax.erf_inv(2.0 * values - 1.0)


def normal_points(first, count, generator, lattice_shift):
    points = first + jnp.arange(count, dtype=jnp.int32)
    residue = (points[:, None] * generator[None, :]) % P_SIZE
    offset = (lattice_shift.astype(jnp.float32) + 0.5) / 1024.0
    uniform = (residue.astype(jnp.float32) + offset[None, :]) / P_SIZE
    return normal_quantile(uniform).astype(jnp.bfloat16)


def reference(generator, lattice_shift, loadings, load_pattern, threshold, exposure, segment_map, net_tiles, net_pattern):
    factors = normal_points(jnp.int32(0), P_SIZE, generator, lattice_shift)
    factor_tiles = factors.reshape(P_SIZE, F // 64, 64)
    blocks_dev = O_DEV // 128

    def shard_loss(carry, index):
        block_start = (index * blocks_dev).astype(jnp.int32)
        row_start = (index * O_DEV).astype(jnp.int32)
        loads = lax.dynamic_slice_in_dim(loadings, block_start, blocks_dev, 0)
        pattern = lax.dynamic_slice_in_dim(load_pattern, block_start, blocks_dev, 0)
        thresh = lax.dynamic_slice_in_dim(threshold, row_start, O_DEV, 0)
        expo = lax.dynamic_slice_in_dim(exposure, row_start, O_DEV, 0)
        segs = lax.dynamic_slice_in_dim(segment_map, row_start, O_DEV, 0)
        picked = factor_tiles[:, pattern].astype(jnp.float32)
        latent = jnp.einsum("pbkf,bkfi->pbi", picked, loads.astype(jnp.float32)).reshape(P_SIZE, O_DEV)
        default_prob = normal_cdf(thresh[None, :] - latent)
        weighted = (expo[None, :] * default_prob).astype(jnp.bfloat16)
        carry = carry + jax.ops.segment_sum(weighted.T.astype(jnp.float32), segs, num_segments=SEGMENTS)
        return carry, None

    seg_loss, _ = lax.scan(shard_loss, jnp.zeros((SEGMENTS, P_SIZE), jnp.float32), jnp.arange(N_WIDE, dtype=jnp.int32))
    loss_blocks = seg_loss.astype(jnp.bfloat16).reshape(SEGMENTS // 128, 128, P_SIZE)
    group_blocks = SEG_DEV // 128
    base = (jnp.arange(SEGMENTS // 128, dtype=jnp.int32) // group_blocks) * group_blocks
    sources = base[:, None] + net_pattern

    def net_block(pair):
        source, tiles = pair
        return jnp.einsum("kjp,kji->pi", loss_blocks[source].astype(jnp.float32), tiles.astype(jnp.float32))

    netted = lax.map(net_block, (sources, net_tiles))
    net_loss = jnp.transpose(netted, (1, 0, 2)).reshape(P_SIZE, SEGMENTS)
    moments = jnp.stack([jnp.mean(net_loss, axis=0), jnp.mean(net_loss * net_loss, axis=0)])
    return (net_loss, moments)
```

```python
import functools

import jax
import jax.numpy as jnp
from jax import lax
from jax.experimental import pallas as pl
from jax.experimental.pallas import tpu as pltpu
from jax.sharding import PartitionSpec as P

P_SIZE = 512
LANES = 128
ROWS = 16
STEP_BLOCKS = 8
DEST_CHUNK = 4

QUANTILE_MID = 2.6095163822174072
QUANTILE = (
    2.883376121520996,
    1.5978178977966309,
    0.023873422294855118,
    -0.0908193290233612,
    0.0662941262125969,
    -0.010339167900383472,
    -0.019267892464995384,
    0.011844170279800892,
    0.003007495542988181,
    -0.004063245374709368,
    -0.00016578214126639068,
    0.0005968576297163963,
)
CDF_SHIFT = 3.0
CDF_MID = 0.1666666716337204
CDF = (
    0.729083776473999,
    3.0559914112091064,
    8.280515670776367,
    10.208822250366211,
    -13.521076202392578,
    -54.16969680786133,
    43.550254821777344,
    285.4417419433594,
    -214.20135498046875,
    -1204.82958984375,
)
HALF_LOG2E = 0.7213475204444817


def horner(coefs, x):
    total = coefs[-1]
    for coef in coefs[-2::-1]:
        total = total * x + coef
    return total


def quantile(scaled):
    x = scaled.astype(jnp.float32) * (2.0**-31)
    s = 2.0 - jnp.log(1.0 - x * x)
    y = s * lax.rsqrt(s)
    return x * horner(QUANTILE, y - QUANTILE_MID)


def weighted_prob(t, exposure):
    y = jnp.abs(t)
    r = lax.rsqrt(y + CDF_SHIFT)
    q = r * r
    tail = jnp.exp2(t * t * -HALF_LOG2E) * q * horner(CDF, q - CDF_MID)
    return exposure * jnp.where(t > 0.0, 1.0 - tail, tail)


def loss_kernel(n_parts, n_dest, split, meta, pattern, *refs):
    parts = refs[:n_parts]
    load_ref, thr_ref, expo_ref, seg_ref = refs[n_parts : n_parts + 4]
    outs = refs[n_parts + 4 : -5]
    panel, acc, weighted, masked, onehot = refs[-5:]
    points = acc.shape[1]
    seg_dev = acc.shape[2]
    step = pl.program_id(0)
    width = parts[0].shape[1]
    columns = width // LANES

    @pl.when(step == 0)
    def _():
        acc[...] = jnp.zeros_like(acc)
        row = lax.broadcasted_iota(jnp.int32, (ROWS, LANES), 0) + meta[0]

        for k in range(n_parts):
            first = meta[2 + k] * columns

            def fill(c, carry, k=k, first=first):
                at = pl.ds(pl.multiple_of(c * LANES, LANES), LANES)
                gen = parts[k][0:1, at]
                shift = parts[k][1:2, at]
                scaled = lax.shift_left(row * gen, 23) + (lax.shift_left(shift, 13) + (4096 - 2**31))
                jump = lax.shift_left(gen, 27)
                for r in range(points // ROWS):
                    value = quantile(scaled)
                    rows = pl.ds(r * ROWS, ROWS)
                    panel[0, first + c, rows, :] = value.astype(jnp.bfloat16)
                    panel[1, first + c, rows, :] = pltpu.roll(value, LANES // 2, 1).astype(jnp.bfloat16)
                    scaled = scaled + jump
                return carry

            lax.fori_loop(0, columns, fill, 0)

    low = lax.broadcasted_iota(jnp.int32, (points, LANES), 1) < LANES // 2
    seg_row = lax.broadcasted_iota(jnp.int32, (seg_dev, LANES), 0)

    def rel_dest(seg):
        dest = lax.shift_right_logical(seg, seg_dev.bit_length() - 1) - meta[1]
        return jnp.where(dest < 0, dest + n_dest, dest)

    for j in range(STEP_BLOCKS):
        b = step * STEP_BLOCKS + j
        here = slice(j * LANES, (j + 1) * LANES)
        halves = []
        for k in (0, 2):
            q0 = pattern[4 * b + k]
            q1 = pattern[4 * b + k + 1]
            left = panel[q0 & 1, lax.shift_right_logical(q0, 1)]
            right = panel[1 - (q1 & 1), lax.shift_right_logical(q1, 1)]
            halves.append(jnp.where(low, left, right))
        picked = jnp.concatenate(halves, axis=1)
        latent = jnp.dot(picked, load_ref[j], preferred_element_type=jnp.float32)
        one = pl.ds(b, 1)
        prob = weighted_prob(thr_ref[one, :] - latent, expo_ref[one, :])
        weighted[:, here] = prob.astype(jnp.bfloat16)
        local = seg_ref[one, :] & (seg_dev - 1)
        onehot[:, here] = jnp.where(seg_row == local, 1.0, 0.0).astype(jnp.bfloat16)

    def add_chunk(chunk):
        for j in range(STEP_BLOCKS):
            here = slice(j * LANES, (j + 1) * LANES)
            dest = rel_dest(seg_ref[pl.ds(step * STEP_BLOCKS + j, 1), :])
            for d in range(split):
                mine = jnp.where(dest == chunk * split + d, 1.0, 0.0).astype(jnp.bfloat16)
                masked[d * points : (d + 1) * points, here] = weighted[:, here] * mine
        sums = lax.dot_general(
            masked[...], onehot[...], (((1,), (1,)), ((), ())), preferred_element_type=jnp.float32
        )
        for d in range(split):
            acc[chunk * split + d] += sums[d * points : (d + 1) * points]

    if n_dest == split:
        add_chunk(0)
    else:
        lax.fori_loop(0, n_dest // split, lambda c, x: (add_chunk(c), x)[1], 0)

    @pl.when(step == pl.num_programs(0) - 1)
    def _():
        for d in range(n_dest):
            if len(outs) == 1:
                outs[0][d] = acc[d].astype(jnp.bfloat16)
            else:
                outs[d][...] = acc[d].astype(jnp.bfloat16)


def net_kernel(pattern, *refs):
    tiles_ref, net_ref, sums_ref, losses = refs[-4:]
    received = refs[:-4]
    blocks = tiles_ref.shape[0]
    slots = tiles_ref.shape[1] // LANES
    for q in range(blocks):
        at = slice(q * LANES, (q + 1) * LANES)
        if len(received) == 1:
            total = jnp.sum(received[0][:, :, at].astype(jnp.float32), axis=0)
        else:
            total = received[0][:, at].astype(jnp.float32)
            for ref in received[1:]:
                total = total + ref[:, at].astype(jnp.float32)
        losses[q] = total.astype(jnp.bfloat16)
    for b in range(blocks):
        at = slice(b * LANES, (b + 1) * LANES)
        picked = jnp.concatenate([losses[pattern[slots * b + k]] for k in range(slots)], axis=1)
        net = jnp.dot(picked, tiles_ref[b], preferred_element_type=jnp.float32)
        net_ref[:, at] = net
        sums_ref[0:1, at] = jnp.sum(net, axis=0, keepdims=True)
        sums_ref[1:2, at] = jnp.sum(net * net, axis=0, keepdims=True)


def shifted(x, axis, k):
    n = lax.axis_size(axis)
    return lax.ppermute(x, axis, [(i, (i + k) % n) for i in range(n)])


def swapped(x, axis, k):
    return lax.ppermute(x, axis, [(i, i ^ k) for i in range(lax.axis_size(axis))])


def pair_sum(terms):
    while len(terms) > 1:
        terms = [terms[i] + terms[i + 1] for i in range(0, len(terms), 2)]
    return terms[0]


def body(
    generator,
    lattice_shift,
    loadings,
    load_pattern,
    threshold,
    exposure,
    segment_map,
    net_tiles,
    net_pattern,
):
    n_narrow = lax.axis_size("narrow")
    n_dest = lax.axis_size("wide")
    me = lax.axis_index("narrow")
    points = P_SIZE // n_narrow
    blocks = loadings.shape[0]
    seg_blocks = net_tiles.shape[0]
    seg_dev = seg_blocks * LANES
    direct = n_dest <= 8
    split = min(n_dest, DEST_CHUNK)

    own = jnp.stack([generator, lattice_shift])
    parts = [own] + [swapped(own, "narrow", k) for k in range(1, n_narrow)]
    quarter = [me ^ k for k in range(n_narrow)]
    base = lax.axis_index("wide") if direct else 0
    meta = jnp.stack([me * points, jnp.int32(base)] + quarter).astype(jnp.int32)

    block = jax.ShapeDtypeStruct((points, seg_dev), jnp.bfloat16)
    whole = lambda *shape: pl.BlockSpec(shape, lambda s, *_: (0,) * len(shape))
    if direct:
        out_shape = [block] * n_dest
        out_specs = [whole(points, seg_dev)] * n_dest
    else:
        out_shape = [jax.ShapeDtypeStruct((n_dest, points, seg_dev), jnp.bfloat16)]
        out_specs = [whole(n_dest, points, seg_dev)]
    step_width = STEP_BLOCKS * LANES
    partial = pl.pallas_call(
        functools.partial(loss_kernel, n_narrow, n_dest, split),
        out_shape=out_shape,
        grid_spec=pltpu.PrefetchScalarGridSpec(
            num_scalar_prefetch=2,
            grid=(blocks // STEP_BLOCKS,),
            in_specs=[whole(*own.shape)] * n_narrow
            + [pl.BlockSpec((STEP_BLOCKS, 256, LANES), lambda s, *_: (s, 0, 0))]
            + [whole(blocks, LANES)] * 3,
            out_specs=out_specs,
            scratch_shapes=[
                pltpu.VMEM((2, own.shape[1] * n_narrow // LANES, points, LANES), jnp.bfloat16),
                pltpu.VMEM((n_dest, points, seg_dev), jnp.float32),
                pltpu.VMEM((points, step_width), jnp.bfloat16),
                pltpu.VMEM((split * points, step_width), jnp.bfloat16),
                pltpu.VMEM((seg_dev, step_width), jnp.bfloat16),
            ],
        ),
        compiler_params=pltpu.CompilerParams(vmem_limit_bytes=60 << 20),
        name="loss",
    )(
        meta,
        load_pattern.reshape(-1),
        *parts,
        loadings.reshape(blocks, 256, LANES),
        threshold.reshape(blocks, LANES),
        exposure.reshape(blocks, LANES),
        segment_map.reshape(blocks, LANES),
    )

    if direct:
        received = [partial[0]] + [shifted(partial[k], "wide", k) for k in range(1, n_dest)]
        received_specs = [pl.BlockSpec(memory_space=pltpu.VMEM)] * n_dest
    else:
        received = [lax.all_to_all(partial[0], "wide", split_axis=0, concat_axis=0, tiled=True)]
        received_specs = [pl.BlockSpec(memory_space=pltpu.VMEM)]
    slots = net_tiles.shape[1]
    net_loss, sums = pl.pallas_call(
        net_kernel,
        out_shape=[
            jax.ShapeDtypeStruct((points, seg_dev), jnp.float32),
            jax.ShapeDtypeStruct((2, seg_dev), jnp.float32),
        ],
        in_specs=[pl.BlockSpec(memory_space=pltpu.SMEM)]
        + received_specs
        + [pl.BlockSpec(memory_space=pltpu.VMEM)],
        out_specs=[pl.BlockSpec(memory_space=pltpu.VMEM)] * 2,
        scratch_shapes=[pltpu.VMEM((seg_blocks, points, LANES), jnp.bfloat16)],
        compiler_params=pltpu.CompilerParams(vmem_limit_bytes=40 << 20),
        name="net",
    )(net_pattern.reshape(-1), *received, net_tiles.reshape(seg_blocks, slots * LANES, LANES))

    total = pair_sum([sums] + [swapped(sums, "narrow", k) for k in range(1, n_narrow)])
    return (net_loss, total / P_SIZE)


def solution(mesh):
    return jax.shard_map(
        body,
        mesh=mesh,
        in_specs=(
            P("narrow"),
            P(("groups", "narrow")),
            P(("groups", "wide"), None, None, None),
            P(("groups", "wide"), None),
            P(("groups", "wide")),
            P(("groups", "wide")),
            P(("groups", "wide")),
            P(("groups", "wide"), None, None, None),
            P(("groups", "wide"), None),
        ),
        out_specs=(P("narrow", ("groups", "wide")), P(None, ("groups", "wide"))),
        check_vma=False,
    )
```

```python
import functools

import jax
import jax.numpy as jnp
from jax import lax
from jax.experimental import pallas as pl
from jax.experimental.pallas import tpu as pltpu
from jax.sharding import PartitionSpec as P

P_SIZE = 512
LANES = 128
ROWS = 16
STEP_BLOCKS = 4
DEST_CHUNK = 4
DOT_ROWS = 512
PIECE = 256
CHUNKS = 2
VMEM_LIMIT = 48 << 20

QUANTILE_MID = 2.6095163822174072
QUANTILE = (
    2.883376121520996,
    1.5978178977966309,
    0.023873422294855118,
    -0.0908193290233612,
    0.0662941262125969,
    -0.010339167900383472,
    -0.019267892464995384,
    0.011844170279800892,
    0.003007495542988181,
    -0.004063245374709368,
    -0.00016578214126639068,
    0.0005968576297163963,
)
CDF_SHIFT = 3.0
CDF_MID = 0.1666666716337204
CDF = (
    0.729083776473999,
    3.0559914112091064,
    8.280515670776367,
    10.208822250366211,
    -13.521076202392578,
    -54.16969680786133,
    43.550254821777344,
    285.4417419433594,
    -214.20135498046875,
    -1204.82958984375,
)
HALF_LOG2E = 0.7213475204444817


def horner(coefs, x):
    total = coefs[-1]
    for coef in coefs[-2::-1]:
        total = total * x + coef
    return total


def quantile(scaled):
    x = scaled.astype(jnp.float32) * (2.0**-31)
    s = 2.0 - jnp.log(1.0 - x * x)
    y = s * lax.rsqrt(s)
    return x * horner(QUANTILE, y - QUANTILE_MID)


def weighted_prob(t, exposure):
    y = jnp.abs(t)
    r = lax.rsqrt(y + CDF_SHIFT)
    q = r * r
    tail = jnp.exp2(t * t * -HALF_LOG2E) * q * horner(CDF, q - CDF_MID)
    return exposure * jnp.where(t > 0.0, 1.0 - tail, tail)


def loss_kernel(n_parts, n_dest, split, sub, direct, first_point, meta, pattern, *refs):
    parts = refs[:n_parts]
    load_ref, thr_ref, expo_ref, seg_ref = refs[n_parts : n_parts + 4]
    outs = refs[n_parts + 4 : -8]
    panel, acc = refs[-8:-6]
    latents = refs[-6:-4]
    slots = (refs[-4:-2], refs[-2:])
    points = acc.shape[1]
    seg_sub = acc.shape[2]
    seg_dev = seg_sub * sub
    blocks = load_ref.shape[0]
    columns = parts[0].shape[1] // LANES
    chunks = n_dest // split
    steps = blocks // STEP_BLOCKS

    acc[...] = jnp.zeros_like(acc)
    row = lax.broadcasted_iota(jnp.int32, (ROWS, LANES), 0) + (meta[0] + first_point)
    for k in range(n_parts):
        first = meta[2 + k] * columns

        def fill(c, carry, k=k, first=first):
            at = pl.ds(pl.multiple_of(c * LANES, LANES), LANES)
            gen = parts[k][0:1, at]
            shift = parts[k][1:2, at]
            scaled = lax.shift_left(row * gen, 23) + (lax.shift_left(shift, 13) + (4096 - 2**31))
            jump = lax.shift_left(gen, 27)
            for r in range(points // ROWS):
                value = quantile(scaled)
                rows = pl.ds(r * ROWS, ROWS)
                panel[0, first + c, rows, :] = value.astype(jnp.bfloat16)
                panel[1, first + c, rows, :] = pltpu.roll(value, LANES // 2, 1).astype(jnp.bfloat16)
                scaled = scaled + jump
            return carry

        lax.fori_loop(0, columns, fill, 0, unroll=2)

    low = lax.broadcasted_iota(jnp.int32, (points, LANES), 1) < LANES // 2
    seg_row = lax.broadcasted_iota(jnp.int32, (seg_sub, LANES), 0)

    def part_of(seg):
        part = lax.shift_right_logical(seg, seg_sub.bit_length() - 1) - meta[1] * sub
        return jnp.where(part < 0, part + n_dest * sub, part)

    def project(b, j, latent):
        halves = []
        for k in (0, 2):
            q0 = pattern[4 * b + k]
            q1 = pattern[4 * b + k + 1]
            left = panel[q0 & 1, lax.shift_right_logical(q0, 1)]
            right = panel[1 - (q1 & 1), lax.shift_right_logical(q1, 1)]
            halves.append(jnp.where(low, left, right))
        picked = jnp.concatenate(halves, axis=1)
        latent[:, j * LANES : (j + 1) * LANES] = jnp.dot(
            picked, load_ref[b], preferred_element_type=jnp.float32
        )

    def weigh(b, j, latent, masked, onehot):
        here = slice(j * LANES, (j + 1) * LANES)
        one = pl.ds(b, 1)
        prob = weighted_prob(thr_ref[one, :] - latent[:, here], expo_ref[one, :]).astype(jnp.bfloat16)
        seg = seg_ref[one, :]
        part = part_of(seg)
        onehot[:, here] = jnp.where(seg_row == (seg & (seg_sub - 1)), 1.0, 0.0).astype(jnp.bfloat16)
        for d in range(n_dest * sub):
            mine = jnp.where(part == d, 1.0, 0.0).astype(jnp.bfloat16)
            masked[d * points : (d + 1) * points, here] = prob * mine

    def add_piece(masked, onehot, first, count, segs):
        sums = lax.dot_general(
            masked[pl.ds(first * points, count * points), :],
            onehot[segs, :],
            (((1,), (1,)), ((), ())),
            preferred_element_type=jnp.float32,
        )
        for d in range(count):
            acc[first + d, :, segs] += sums[d * points : (d + 1) * points]

    group = split * sub
    pieces = [
        slice(i * PIECE, (i + 1) * PIECE) for i in range(seg_sub // PIECE)
    ]

    def add_all(masked, onehot):
        for segs in pieces:
            if chunks == 1:
                add_piece(masked, onehot, 0, group, segs)
            else:
                lax.fori_loop(
                    0, chunks, lambda c, x: (add_piece(masked, onehot, c * group, group, segs), x)[1], 0
                )

    def stage(step, new, ahead=True, behind=True):
        old = 1 - new
        waiting = list(pieces) if behind and chunks == 1 else []
        each = -(-STEP_BLOCKS // max(len(waiting), 1))
        for j in range(STEP_BLOCKS):
            if ahead:
                project((step + 1) * STEP_BLOCKS + j, j, latents[old])
            if waiting and j % each == 0:
                add_piece(*slots[old], 0, group, waiting.pop(0))
            weigh(step * STEP_BLOCKS + j, j, latents[new], *slots[new])
        for segs in waiting:
            add_piece(*slots[old], 0, group, segs)
        if behind and chunks > 1:
            add_all(*slots[old])

    for j in range(STEP_BLOCKS):
        project(j, j, latents[0])
    stage(0, 0, behind=False)

    def pair(i, carry):
        stage(2 * i + 1, 1)
        stage(2 * i + 2, 0)
        return carry

    lax.fori_loop(0, steps // 2 - 1, pair, 0)
    stage(steps - 1, 1, ahead=False)
    add_all(*slots[1])

    for d in range(n_dest):
        for i in range(sub):
            at = slice(i * seg_sub, (i + 1) * seg_sub)
            value = acc[d * sub + i]
            if not direct:
                outs[0][d, :, at] = value.astype(jnp.bfloat16)
            else:
                outs[d][:, at] = value.astype(outs[d].dtype)


def net_kernel(n_chunks, pattern, *refs):
    tiles_ref, net_ref, sums_ref, losses = refs[-4:]
    received = refs[:-4]
    blocks = tiles_ref.shape[0]
    slots = tiles_ref.shape[1] // LANES
    count = len(received) // n_chunks
    points = losses.shape[1] // n_chunks
    for c in range(n_chunks):
        mine = received[c * count : (c + 1) * count]
        for q in range(blocks):
            at = slice(q * LANES, (q + 1) * LANES)
            if count == 1:
                total = jnp.sum(mine[0][:, :, at].astype(jnp.float32), axis=0)
            else:
                total = mine[0][:, at]
                for ref in mine[1:]:
                    total = total + ref[:, at].astype(jnp.float32)
            losses[q, c * points : (c + 1) * points] = total.astype(jnp.bfloat16)
    for b in range(blocks):
        at = slice(b * LANES, (b + 1) * LANES)
        picked = jnp.concatenate([losses[pattern[slots * b + k]] for k in range(slots)], axis=1)
        net = jnp.dot(picked, tiles_ref[b], preferred_element_type=jnp.float32)
        net_ref[:, at] = net
        sums_ref[0:1, at] = jnp.sum(net, axis=0, keepdims=True)
        sums_ref[1:2, at] = jnp.sum(net * net, axis=0, keepdims=True)


def loss_call(meta, pattern, parts, loadings, threshold, exposure, segment_map, n_dest, first_point, points, seg_dev, direct):
    blocks = loadings.shape[0]
    own = parts[0]
    n_parts = len(parts)
    split = min(n_dest, DEST_CHUNK)
    sub = max(1, DOT_ROWS // (split * points))
    if direct:
        out_shape = [
            jax.ShapeDtypeStruct((points, seg_dev), jnp.bfloat16 if d else jnp.float32)
            for d in range(n_dest)
        ]
    else:
        out_shape = [jax.ShapeDtypeStruct((n_dest, points, seg_dev), jnp.bfloat16)]
    width = STEP_BLOCKS * LANES
    seg_sub = seg_dev // sub
    slot = [
        pltpu.VMEM((n_dest * sub * points, width), jnp.bfloat16),
        pltpu.VMEM((seg_sub, width), jnp.bfloat16),
    ]
    vmem = pl.BlockSpec(memory_space=pltpu.VMEM)
    smem = pl.BlockSpec(memory_space=pltpu.SMEM)
    return pl.pallas_call(
        functools.partial(loss_kernel, n_parts, n_dest, split, sub, direct, first_point),
        out_shape=out_shape,
        in_specs=[smem, smem] + [vmem] * (n_parts + 4),
        out_specs=[vmem] * len(out_shape),
        scratch_shapes=[
            pltpu.VMEM((2, own.shape[1] * n_parts // LANES, points, LANES), jnp.bfloat16),
            pltpu.VMEM((n_dest * sub, points, seg_sub), jnp.float32),
            pltpu.VMEM((points, width), jnp.float32),
            pltpu.VMEM((points, width), jnp.float32),
        ]
        + slot * 2,
        compiler_params=pltpu.CompilerParams(vmem_limit_bytes=VMEM_LIMIT),
        name="loss",
    )(
        meta,
        pattern,
        *parts,
        loadings.reshape(blocks, 256, LANES),
        threshold.reshape(blocks, LANES),
        exposure.reshape(blocks, LANES),
        segment_map.reshape(blocks, LANES),
    )


def shifted(x, axis, k):
    n = lax.axis_size(axis)
    return lax.ppermute(x, axis, [(i, (i + k) % n) for i in range(n)])


def swapped(x, axis, k):
    return lax.ppermute(x, axis, [(i, i ^ k) for i in range(lax.axis_size(axis))])


def pair_sum(terms):
    while len(terms) > 1:
        terms = [terms[i] + terms[i + 1] for i in range(0, len(terms), 2)]
    return terms[0]


def body(
    generator,
    lattice_shift,
    loadings,
    load_pattern,
    threshold,
    exposure,
    segment_map,
    net_tiles,
    net_pattern,
):
    n_narrow = lax.axis_size("narrow")
    n_dest = lax.axis_size("wide")
    me = lax.axis_index("narrow")
    points = P_SIZE // n_narrow
    seg_blocks = net_tiles.shape[0]
    seg_dev = seg_blocks * LANES
    direct = n_dest <= 8

    own = jnp.stack([generator, lattice_shift])
    parts = [own] + [swapped(own, "narrow", k) for k in range(1, n_narrow)]
    quarter = [me ^ k for k in range(n_narrow)]
    base = lax.axis_index("wide") if direct else 0
    meta = jnp.stack([me * points, jnp.int32(base)] + quarter).astype(jnp.int32)

    slots = net_tiles.shape[1]
    tiles = net_tiles.reshape(seg_blocks, slots * LANES, LANES)
    chunk = points // CHUNKS
    net_loss, sums = None, None
    partials = [
        loss_call(
            meta,
            load_pattern.reshape(-1),
            parts,
            loadings,
            threshold,
            exposure,
            segment_map,
            n_dest,
            c * chunk,
            chunk,
            seg_dev,
            direct,
        )
        for c in range(CHUNKS)
    ]
    received = []
    for partial in partials:
        if direct:
            received += [partial[0]] + [shifted(partial[k], "wide", k) for k in range(1, n_dest)]
        else:
            received += [lax.all_to_all(partial[0], "wide", split_axis=0, concat_axis=0, tiled=True)]
    vmem = pl.BlockSpec(memory_space=pltpu.VMEM)
    net_loss, sums = pl.pallas_call(
        functools.partial(net_kernel, CHUNKS),
        out_shape=[
            jax.ShapeDtypeStruct((points, seg_dev), jnp.float32),
            jax.ShapeDtypeStruct((2, seg_dev), jnp.float32),
        ],
        in_specs=[pl.BlockSpec(memory_space=pltpu.SMEM)] + [vmem] * (len(received) + 1),
        out_specs=[vmem] * 2,
        scratch_shapes=[pltpu.VMEM((seg_blocks, points, LANES), jnp.bfloat16)],
        compiler_params=pltpu.CompilerParams(vmem_limit_bytes=VMEM_LIMIT),
        name="net",
    )(net_pattern.reshape(-1), *received, tiles)

    total = pair_sum([sums] + [swapped(sums, "narrow", k) for k in range(1, n_narrow)])
    return (net_loss, total / P_SIZE)


def solution(mesh):
    return jax.shard_map(
        body,
        mesh=mesh,
        in_specs=(
            P("narrow"),
            P(("groups", "narrow")),
            P(("groups", "wide"), None, None, None),
            P(("groups", "wide"), None),
            P(("groups", "wide")),
            P(("groups", "wide")),
            P(("groups", "wide")),
            P(("groups", "wide"), None, None, None),
            P(("groups", "wide"), None),
        ),
        out_specs=(P("narrow", ("groups", "wide")), P(None, ("groups", "wide"))),
        check_vma=False,
    )
```

```python
import functools

import jax
import jax.numpy as jnp
from jax import lax
from jax.experimental import pallas as pl
from jax.experimental.pallas import tpu as pltpu
from jax.sharding import PartitionSpec as P

P_SIZE = 512
LANES = 128
ROWS = 16
DEST_CHUNK = 4
MXU = 256
CHUNKS = 2
VMEM_LIMIT = 48 << 20

QUANTILE_MID = 2.6095163822174072
QUANTILE = (
    2.883376121520996,
    1.5978178977966309,
    0.023873422294855118,
    -0.0908193290233612,
    0.0662941262125969,
    -0.010339167900383472,
    -0.019267892464995384,
    0.011844170279800892,
    0.003007495542988181,
    -0.004063245374709368,
    -0.00016578214126639068,
    0.0005968576297163963,
)
CDF_SHIFT = 3.0
CDF_MID = 0.1666666716337204
CDF = (
    0.729083776473999,
    3.0559914112091064,
    8.280515670776367,
    10.208822250366211,
    -13.521076202392578,
    -54.16969680786133,
    43.550254821777344,
    285.4417419433594,
    -214.20135498046875,
    -1204.82958984375,
)
HALF_LOG2E = 0.7213475204444817


def horner(coefs, x):
    total = coefs[-1]
    for coef in coefs[-2::-1]:
        total = total * x + coef
    return total


def quantile(scaled):
    x = scaled.astype(jnp.float32) * (2.0**-31)
    s = 2.0 - jnp.log(1.0 - x * x)
    y = s * lax.rsqrt(s)
    return x * horner(QUANTILE, y - QUANTILE_MID)


def weighted_prob(t, exposure):
    y = jnp.abs(t)
    r = lax.rsqrt(y + CDF_SHIFT)
    q = r * r
    tail = jnp.exp2(t * t * -HALF_LOG2E) * q * horner(CDF, q - CDF_MID)
    return exposure * jnp.where(t > 0.0, 1.0 - tail, tail)


def loss_kernel(n_parts, n_dest, split, direct, first_point, meta, pattern, *refs):
    parts = refs[:n_parts]
    sources = refs[n_parts : n_parts + 4]
    outs = refs[n_parts + 4 : -8]
    panel, load_ref, thr_ref, expo_ref, seg_ref, even, odd, sems = refs[-8:]
    masked = (even, odd)
    points = panel.shape[2]
    blocks = load_ref.shape[0]
    columns = parts[0].shape[1] // LANES
    seg_dev = (outs[0] if direct else outs[0].at[0]).shape[1]
    sub = seg_dev // (2 * MXU)
    group = split * sub
    steps = blocks // 2

    copies = [
        pltpu.make_async_copy(source, target, sems.at[i])
        for i, (source, target) in enumerate(zip(sources, (load_ref, thr_ref, expo_ref, seg_ref)))
    ]
    for copy in copies:
        copy.start()

    row = lax.broadcasted_iota(jnp.int32, (ROWS, LANES), 0) + (meta[0] + first_point)
    for k in range(n_parts):
        first = meta[2 + k] * columns

        def fill(c, carry, k=k, first=first):
            at = pl.ds(pl.multiple_of(c * LANES, LANES), LANES)
            gen = parts[k][0:1, at]
            shift = parts[k][1:2, at]
            scaled = lax.shift_left(row * gen, 23) + (lax.shift_left(shift, 13) + (4096 - 2**31))
            jump = lax.shift_left(gen, 27)
            for r in range(points // ROWS):
                value = quantile(scaled)
                rows = pl.ds(r * ROWS, ROWS)
                panel[0, first + c, rows, :] = value.astype(jnp.bfloat16)
                panel[1, first + c, rows, :] = pltpu.roll(value, LANES // 2, 1).astype(jnp.bfloat16)
                scaled = scaled + jump
            return carry

        lax.fori_loop(0, columns, fill, 0, unroll=8)

    for copy in copies:
        copy.wait()

    low = lax.broadcasted_iota(jnp.int32, (points, LANES), 1) < LANES // 2
    seg_row = lax.broadcasted_iota(jnp.int32, (MXU, LANES), 0)

    def picked(b):
        halves = []
        for k in (0, 2):
            q0 = pattern[4 * b + k]
            q1 = pattern[4 * b + k + 1]
            left = panel[q0 & 1, lax.shift_right_logical(q0, 1)]
            right = panel[1 - (q1 & 1), lax.shift_right_logical(q1, 1)]
            halves.append(jnp.where(low, left, right))
        return jnp.concatenate(halves, axis=1)

    def one_pass(chunk, sums, latents):
        def project(step, parity):
            b = 2 * step
            loads = jnp.concatenate([load_ref[b], load_ref[b + 1]], axis=1)
            pltpu.matmul_push_rhs(loads, parity, parity)
            pltpu.matmul_acc_lhs(
                latents[parity], jnp.concatenate([picked(b), picked(b + 1)], axis=0), parity
            )

        def push_onehot(step, parity):
            local = [seg_ref[pl.ds(2 * step + j, 1), :] & (2 * MXU - 1) for j in range(2)]
            for n in range(2):
                tile = [jnp.where(seg_row == at - n * MXU, 1.0, 0.0).astype(jnp.bfloat16) for at in local]
                pltpu.matmul_push_rhs(jnp.concatenate(tile, axis=1), parity, n, transpose=True)

        def add_up(parity):
            for n in range(2):
                pltpu.matmul_acc_lhs(sums[n], masked[parity][...], parity)

        def weigh(step, parity):
            latent = pltpu.matmul_pop(latents[parity])
            for j in range(2):
                one = pl.ds(2 * step + j, 1)
                here = slice(j * LANES, (j + 1) * LANES)
                t = thr_ref[one, :] - latent[j * points : (j + 1) * points, here]
                prob = weighted_prob(t, expo_ref[one, :]).astype(jnp.bfloat16)
                part = lax.shift_right_logical(seg_ref[one, :], (2 * MXU).bit_length() - 1) - meta[1] * sub
                part = jnp.where(part < 0, part + n_dest * sub, part) - chunk * group
                for d in range(group):
                    mine = jnp.where(part == d, 1.0, 0.0).astype(jnp.bfloat16)
                    masked[parity][d * points : (d + 1) * points, here] = prob * mine

        def stage(step, parity, ahead=True, behind=True):
            push_onehot(step, parity)
            if behind:
                add_up(1 - parity)
            if ahead:
                project(step + 1, 1 - parity)
            weigh(step, parity)

        project(0, 0)
        stage(0, 0, behind=False)

        def pair(i, carry):
            stage(2 * i + 1, 1)
            stage(2 * i + 2, 0)
            return carry

        lax.fori_loop(0, steps // 2 - 1, pair, 0)
        stage(steps - 1, 1, ahead=False)
        add_up(1)

        for n in range(2):
            total = pltpu.matmul_pop(sums[n])
            for d in range(split):
                for i in range(sub):
                    at = slice(i * 2 * MXU + n * MXU, i * 2 * MXU + (n + 1) * MXU)
                    value = total[(d * sub + i) * points : (d * sub + i + 1) * points]
                    if direct:
                        outs[d][:, at] = value.astype(outs[d].dtype)
                    else:
                        outs[0][chunk * split + d, :, at] = value.astype(jnp.bfloat16)

    def passes(*accs):
        if n_dest == split:
            one_pass(0, accs[:2], accs[2:])
        else:
            lax.fori_loop(0, n_dest // split, lambda c, x: (one_pass(c, accs[:2], accs[2:]), x)[1], 0)

    pl.run_scoped(
        passes,
        *[pltpu.ACC(n)((group * points, MXU), jnp.float32) for n in range(2)],
        *[pltpu.ACC(n)((2 * points, MXU), jnp.float32) for n in range(2)],
    )


def net_kernel(n_chunks, pattern, *refs):
    tiles_ref, net_ref, sums_ref, losses = refs[-4:]
    received = refs[:-4]
    blocks = tiles_ref.shape[0]
    slots = tiles_ref.shape[1] // LANES
    count = len(received) // n_chunks
    points = losses.shape[1] // n_chunks
    for c in range(n_chunks):
        mine = received[c * count : (c + 1) * count]
        for q in range(blocks):
            at = slice(q * LANES, (q + 1) * LANES)
            if count == 1:
                total = jnp.sum(mine[0][:, :, at].astype(jnp.float32), axis=0)
            else:
                total = mine[0][:, at]
                for ref in mine[1:]:
                    total = total + ref[:, at].astype(jnp.float32)
            losses[q, c * points : (c + 1) * points] = total.astype(jnp.bfloat16)
    for b in range(blocks):
        at = slice(b * LANES, (b + 1) * LANES)
        picked = jnp.concatenate([losses[pattern[slots * b + k]] for k in range(slots)], axis=1)
        net = jnp.dot(picked, tiles_ref[b], preferred_element_type=jnp.float32)
        net_ref[:, at] = net
        sums_ref[0:1, at] = jnp.sum(net, axis=0, keepdims=True)
        sums_ref[1:2, at] = jnp.sum(net * net, axis=0, keepdims=True)


def loss_call(meta, pattern, parts, loadings, threshold, exposure, segment_map, n_dest, first_point, points, seg_dev, direct):
    blocks = loadings.shape[0]
    own = parts[0]
    n_parts = len(parts)
    split = min(n_dest, DEST_CHUNK)
    if direct:
        out_shape = [
            jax.ShapeDtypeStruct((points, seg_dev), jnp.bfloat16 if d else jnp.float32)
            for d in range(n_dest)
        ]
    else:
        out_shape = [jax.ShapeDtypeStruct((n_dest, points, seg_dev), jnp.bfloat16)]
    slot = pltpu.VMEM((split * seg_dev // (2 * MXU) * points, MXU), jnp.bfloat16)
    vmem = pl.BlockSpec(memory_space=pltpu.VMEM)
    smem = pl.BlockSpec(memory_space=pltpu.SMEM)
    hbm = pl.BlockSpec(memory_space=pl.ANY)
    return pl.pallas_call(
        functools.partial(loss_kernel, n_parts, n_dest, split, direct, first_point),
        out_shape=out_shape,
        in_specs=[smem, smem] + [vmem] * n_parts + [hbm] * 4,
        out_specs=[vmem] * len(out_shape),
        scratch_shapes=[
            pltpu.VMEM((2, own.shape[1] * n_parts // LANES, points, LANES), jnp.bfloat16),
            pltpu.VMEM((blocks, 256, LANES), jnp.bfloat16),
            pltpu.VMEM((blocks, LANES), jnp.float32),
            pltpu.VMEM((blocks, LANES), jnp.float32),
            pltpu.VMEM((blocks, LANES), jnp.int32),
            slot,
            slot,
            pltpu.SemaphoreType.DMA((4,)),
        ],
        compiler_params=pltpu.CompilerParams(vmem_limit_bytes=VMEM_LIMIT),
        name="loss",
    )(
        meta,
        pattern,
        *parts,
        loadings.reshape(blocks, 256, LANES),
        threshold.reshape(blocks, LANES),
        exposure.reshape(blocks, LANES),
        segment_map.reshape(blocks, LANES),
    )


def shifted(x, axis, k):
    n = lax.axis_size(axis)
    return lax.ppermute(x, axis, [(i, (i + k) % n) for i in range(n)])


def swapped(x, axis, k):
    return lax.ppermute(x, axis, [(i, i ^ k) for i in range(lax.axis_size(axis))])


def pair_sum(terms):
    while len(terms) > 1:
        terms = [terms[i] + terms[i + 1] for i in range(0, len(terms), 2)]
    return terms[0]


def body(
    generator,
    lattice_shift,
    loadings,
    load_pattern,
    threshold,
    exposure,
    segment_map,
    net_tiles,
    net_pattern,
):
    n_narrow = lax.axis_size("narrow")
    n_dest = lax.axis_size("wide")
    me = lax.axis_index("narrow")
    points = P_SIZE // n_narrow
    seg_blocks = net_tiles.shape[0]
    seg_dev = seg_blocks * LANES
    direct = n_dest <= 8

    own = jnp.stack([generator, lattice_shift])
    parts = [own] + [swapped(own, "narrow", k) for k in range(1, n_narrow)]
    quarter = [me ^ k for k in range(n_narrow)]
    base = lax.axis_index("wide") if direct else 0
    meta = jnp.stack([me * points, jnp.int32(base)] + quarter).astype(jnp.int32)

    slots = net_tiles.shape[1]
    tiles = net_tiles.reshape(seg_blocks, slots * LANES, LANES)
    chunk = points // CHUNKS
    net_loss, sums = None, None
    partials = [
        loss_call(
            meta,
            load_pattern.reshape(-1),
            parts,
            loadings,
            threshold,
            exposure,
            segment_map,
            n_dest,
            c * chunk,
            chunk,
            seg_dev,
            direct,
        )
        for c in range(CHUNKS)
    ]
    received = []
    for partial in partials:
        if direct:
            received += [partial[0]] + [shifted(partial[k], "wide", k) for k in range(1, n_dest)]
        else:
            received += [lax.all_to_all(partial[0], "wide", split_axis=0, concat_axis=0, tiled=True)]
    vmem = pl.BlockSpec(memory_space=pltpu.VMEM)
    net_loss, sums = pl.pallas_call(
        functools.partial(net_kernel, CHUNKS),
        out_shape=[
            jax.ShapeDtypeStruct((points, seg_dev), jnp.float32),
            jax.ShapeDtypeStruct((2, seg_dev), jnp.float32),
        ],
        in_specs=[pl.BlockSpec(memory_space=pltpu.SMEM)] + [vmem] * (len(received) + 1),
        out_specs=[vmem] * 2,
        scratch_shapes=[pltpu.VMEM((seg_blocks, points, LANES), jnp.bfloat16)],
        compiler_params=pltpu.CompilerParams(vmem_limit_bytes=VMEM_LIMIT),
        name="net",
    )(net_pattern.reshape(-1), *received, tiles)

    total = pair_sum([sums] + [swapped(sums, "narrow", k) for k in range(1, n_narrow)])
    return (net_loss, total / P_SIZE)


def solution(mesh):
    return jax.shard_map(
        body,
        mesh=mesh,
        in_specs=(
            P("narrow"),
            P(("groups", "narrow")),
            P(("groups", "wide"), None, None, None),
            P(("groups", "wide"), None),
            P(("groups", "wide")),
            P(("groups", "wide")),
            P(("groups", "wide")),
            P(("groups", "wide"), None, None, None),
            P(("groups", "wide"), None),
        ),
        out_specs=(P("narrow", ("groups", "wide")), P(None, ("groups", "wide"))),
        check_vma=False,
    )
```

```python
import functools

import jax
import jax.numpy as jnp
from jax import lax
from jax.experimental import pallas as pl
from jax.experimental.pallas import tpu as pltpu
from jax.sharding import PartitionSpec as P

P_SIZE = 512
LANES = 128
ROWS = 16
DEST_CHUNK = 4
MXU = 256
CHUNKS = (64, 64)
VMEM_LIMIT = 48 << 20
NET_VMEM = 24 << 20

QUANTILE_MID = 2.6095163822174072
QUANTILE = (
    2.883376121520996,
    1.5978178977966309,
    0.023873422294855118,
    -0.0908193290233612,
    0.0662941262125969,
    -0.010339167900383472,
    -0.019267892464995384,
    0.011844170279800892,
    0.003007495542988181,
    -0.004063245374709368,
    -0.00016578214126639068,
    0.0005968576297163963,
)
CDF_SHIFT = 3.0
CDF_MID = 0.1666666716337204
CDF = (
    0.729083776473999,
    3.0559914112091064,
    8.280515670776367,
    10.208822250366211,
    -13.521076202392578,
    -54.16969680786133,
    43.550254821777344,
    285.4417419433594,
    -214.20135498046875,
    -1204.82958984375,
)
HALF_LOG2E = 0.7213475204444817


def horner(coefs, x):
    total = coefs[-1]
    for coef in coefs[-2::-1]:
        total = total * x + coef
    return total


def quantile(scaled):
    x = scaled.astype(jnp.float32) * (2.0**-31)
    s = 2.0 - jnp.log(1.0 - x * x)
    y = s * lax.rsqrt(s)
    return x * horner(QUANTILE, y - QUANTILE_MID)


def weighted_prob(t, exposure):
    y = jnp.abs(t)
    r = lax.rsqrt(y + CDF_SHIFT)
    q = r * r
    tail = jnp.exp2(t * t * -HALF_LOG2E) * q * horner(CDF, q - CDF_MID)
    return exposure * jnp.where(t > 0.0, 1.0 - tail, tail)


def fill_panel(panel, first, part, first_point):
    points = panel.shape[2]
    row = lax.broadcasted_iota(jnp.int32, (ROWS, LANES), 0) + first_point

    def fill(c, carry):
        at = pl.ds(pl.multiple_of(c * LANES, LANES), LANES)
        gen = part[0:1, at]
        shift = part[1:2, at]
        scaled = lax.shift_left(row * gen, 23) + (lax.shift_left(shift, 13) + (4096 - 2**31))
        jump = lax.shift_left(gen, 27)
        for r in range(points // ROWS):
            value = quantile(scaled).astype(jnp.bfloat16)
            rows = pl.ds(r * ROWS, ROWS)
            panel[0, first + c, rows, :] = value
            panel[1, first + c, rows, :] = pltpu.roll(value, LANES // 2, 1)
            scaled = scaled + jump
        return carry

    lax.fori_loop(0, part.shape[1] // LANES, fill, 0, unroll=max(1, 1024 // points))


def panel_kernel(meta, part, panel):
    fill_panel(panel, 0, part, meta[0])


def loss_kernel(n_parts, n_dest, split, direct, first_point, meta, pattern, *refs):
    own_panel = refs[0]
    parts = refs[1:n_parts]
    sources = refs[n_parts : n_parts + 4]
    outs = refs[n_parts + 4 : -8]
    panel, load_ref, thr_ref, expo_ref, seg_ref, even, odd, sems = refs[-8:]
    masked = (even, odd)
    points = panel.shape[2]
    blocks = load_ref.shape[0]
    columns = own_panel.shape[1]
    seg_dev = (outs[0] if direct else outs[0].at[0]).shape[1]
    sub = seg_dev // (2 * MXU)
    group = split * sub
    steps = blocks // 2

    copies = [
        pltpu.make_async_copy(source, target, sems.at[i])
        for i, (source, target) in enumerate(zip(sources, (load_ref, thr_ref, expo_ref, seg_ref)))
    ]
    for copy in copies:
        copy.start()

    def reuse(c, carry):
        panel[:, meta[2] * columns + c] = own_panel[:, c, first_point : first_point + points, :]
        return carry

    lax.fori_loop(0, columns, reuse, 0, unroll=4)
    for k in range(1, n_parts):
        fill_panel(panel, meta[2 + k] * columns, parts[k - 1], meta[0] + first_point)

    for copy in copies:
        copy.wait()

    low = lax.broadcasted_iota(jnp.int32, (points, LANES), 1) < LANES // 2
    seg_row = lax.broadcasted_iota(jnp.int32, (ROWS, LANES), 0)

    def picked(b):
        halves = []
        for k in (0, 2):
            q0 = pattern[4 * b + k]
            q1 = pattern[4 * b + k + 1]
            left = panel[q0 & 1, lax.shift_right_logical(q0, 1)]
            right = panel[1 - (q1 & 1), lax.shift_right_logical(q1, 1)]
            halves.append(jnp.where(low, left, right))
        return jnp.concatenate(halves, axis=1)

    def one_pass(chunk, sums, latents):
        def project(step, parity):
            b = 2 * step
            loads = jnp.concatenate([load_ref[b], load_ref[b + 1]], axis=1)
            pltpu.matmul_push_rhs(loads, parity, parity)
            pltpu.matmul_acc_lhs(
                latents[parity], jnp.concatenate([picked(b), picked(b + 1)], axis=0), parity
            )

        def push_onehot(step, parity):
            local = [seg_ref[pl.ds(2 * step + j, 1), :] & (2 * MXU - 1) for j in range(2)]
            low_rows = [jnp.where(seg_row == (at & (ROWS - 1)), 1.0, 0.0).astype(jnp.bfloat16) for at in local]
            high = [
                jnp.broadcast_to(lax.shift_right_logical(at, 4), (ROWS, LANES)).astype(jnp.int16)
                for at in local
            ]
            for n in range(2):
                tile = [
                    jnp.concatenate(
                        [
                            jnp.where(high[j] == jnp.int16(n * MXU // ROWS + r), low_rows[j], jnp.bfloat16(0))
                            for r in range(MXU // ROWS)
                        ],
                        axis=0,
                    )
                    for j in range(2)
                ]
                pltpu.matmul_push_rhs(jnp.concatenate(tile, axis=1), parity, n, transpose=True)

        def add_up(parity):
            for n in range(2):
                pltpu.matmul_acc_lhs(sums[n], masked[parity][...], parity)

        def weigh(step, parity):
            latent = pltpu.matmul_pop(latents[parity])
            for j in range(2):
                one = pl.ds(2 * step + j, 1)
                here = slice(j * LANES, (j + 1) * LANES)
                t = thr_ref[one, :] - latent[j * points : (j + 1) * points, here]
                prob = weighted_prob(t, expo_ref[one, :]).astype(jnp.bfloat16)
                part = lax.shift_right_logical(seg_ref[one, :], (2 * MXU).bit_length() - 1) - meta[1] * sub
                part = jnp.where(part < 0, part + n_dest * sub, part) - chunk * group
                part = jnp.broadcast_to(part, (ROWS, LANES)).astype(jnp.int16)
                for d in range(group):
                    mine = part == jnp.int16(d)
                    for r in range(0, points, ROWS):
                        masked[parity][d * points + r : d * points + r + ROWS, here] = jnp.where(
                            mine, prob[r : r + ROWS], jnp.bfloat16(0)
                        )

        def stage(step, parity, ahead=True, behind=True):
            push_onehot(step, parity)
            if behind:
                add_up(1 - parity)
            if ahead:
                project(step + 1, 1 - parity)
            weigh(step, parity)

        project(0, 0)
        stage(0, 0, behind=False)

        def pair(i, carry):
            stage(2 * i + 1, 1)
            stage(2 * i + 2, 0)
            return carry

        lax.fori_loop(0, steps // 2 - 1, pair, 0)
        stage(steps - 1, 1, ahead=False)
        add_up(1)

        for n in range(2):
            total = pltpu.matmul_pop(sums[n])
            for d in range(split):
                for i in range(sub):
                    at = slice(i * 2 * MXU + n * MXU, i * 2 * MXU + (n + 1) * MXU)
                    value = total[(d * sub + i) * points : (d * sub + i + 1) * points]
                    if direct:
                        outs[d][:, at] = value.astype(outs[d].dtype)
                    else:
                        outs[0][chunk * split + d, :, at] = value.astype(jnp.bfloat16)

    def passes(*accs):
        if n_dest == split:
            one_pass(0, accs[:2], accs[2:])
        else:
            lax.fori_loop(0, n_dest // split, lambda c, x: (one_pass(c, accs[:2], accs[2:]), x)[1], 0)

    pl.run_scoped(
        passes,
        *[pltpu.ACC(n)((group * points, MXU), jnp.float32) for n in range(2)],
        *[pltpu.ACC(n)((2 * points, MXU), jnp.float32) for n in range(2)],
    )


def net_kernel(first_point, n_received, pattern, tiles_ref, *refs):
    received = refs[:n_received]
    out_ref, sums_ref, losses, net_rows, sem = refs[-5:]
    before = refs[n_received : -5]
    blocks = tiles_ref.shape[0]
    points = losses.shape[1]
    slots = tiles_ref.shape[1] // LANES
    for q in range(blocks):
        at = slice(q * LANES, (q + 1) * LANES)
        if n_received == 1:
            total = jnp.sum(received[0][:, :, at].astype(jnp.float32), axis=0)
        else:
            total = received[0][:, at].astype(jnp.float32)
            for ref in received[1:]:
                total = total + ref[:, at].astype(jnp.float32)
        losses[q] = total.astype(jnp.bfloat16)
    for b in range(blocks):
        at = slice(b * LANES, (b + 1) * LANES)
        picked = jnp.concatenate([losses[pattern[slots * b + k]] for k in range(slots)], axis=1)
        net = jnp.dot(picked, tiles_ref[b], preferred_element_type=jnp.float32)
        net_rows[:, at] = net
        first = jnp.sum(net, axis=0, keepdims=True)
        second = jnp.sum(net * net, axis=0, keepdims=True)
        if before:
            first += before[0][0:1, at]
            second += before[0][1:2, at]
        sums_ref[0:1, at] = first
        sums_ref[1:2, at] = second
    copy = pltpu.make_async_copy(net_rows, out_ref.at[pl.ds(first_point, points), :], sem)
    copy.start()
    copy.wait()


def net_call(net_pattern, tiles, received, first_point, chunk, points, seg_dev, before):
    vmem = pl.BlockSpec(memory_space=pltpu.VMEM)
    hbm = pl.BlockSpec(memory_space=pltpu.HBM)
    extra = [] if before is None else [before[1], before[0]]
    return pl.pallas_call(
        functools.partial(net_kernel, first_point, len(received)),
        out_shape=[
            jax.ShapeDtypeStruct((points, seg_dev), jnp.float32),
            jax.ShapeDtypeStruct((2, seg_dev), jnp.float32),
        ],
        in_specs=[pl.BlockSpec(memory_space=pltpu.SMEM)]
        + [vmem] * (1 + len(received))
        + [vmem, hbm][: len(extra)],
        out_specs=[hbm, vmem],
        scratch_shapes=[
            pltpu.VMEM((seg_dev // LANES, chunk, LANES), jnp.bfloat16),
            pltpu.VMEM((chunk, seg_dev), jnp.float32),
            pltpu.SemaphoreType.DMA,
        ],
        input_output_aliases={} if before is None else {3 + len(received): 0},
        compiler_params=pltpu.CompilerParams(vmem_limit_bytes=NET_VMEM),
        name="net",
    )(net_pattern, tiles, *received, *extra)


def loss_call(meta, pattern, own_panel, parts, loadings, threshold, exposure, segment_map, n_dest, first_point, points, seg_dev, direct):
    blocks = loadings.shape[0]
    n_parts = len(parts) + 1
    columns = own_panel.shape[1] * n_parts
    split = min(n_dest, DEST_CHUNK)
    if direct:
        out_shape = [
            jax.ShapeDtypeStruct((points, seg_dev), jnp.bfloat16 if d else jnp.float32)
            for d in range(n_dest)
        ]
    else:
        out_shape = [jax.ShapeDtypeStruct((n_dest, points, seg_dev), jnp.bfloat16)]
    slot = pltpu.VMEM((split * seg_dev // (2 * MXU) * points, MXU), jnp.bfloat16)
    vmem = pl.BlockSpec(memory_space=pltpu.VMEM)
    smem = pl.BlockSpec(memory_space=pltpu.SMEM)
    hbm = pl.BlockSpec(memory_space=pltpu.HBM)
    return pl.pallas_call(
        functools.partial(loss_kernel, n_parts, n_dest, split, direct, first_point),
        out_shape=out_shape,
        in_specs=[smem, smem] + [vmem] * n_parts + [hbm] * 4,
        out_specs=[vmem] * len(out_shape),
        scratch_shapes=[
            pltpu.VMEM((2, columns, points, LANES), jnp.bfloat16),
            pltpu.VMEM((blocks, 256, LANES), jnp.bfloat16),
            pltpu.VMEM((blocks, LANES), jnp.float32),
            pltpu.VMEM((blocks, LANES), jnp.float32),
            pltpu.VMEM((blocks, LANES), jnp.int32),
            slot,
            slot,
            pltpu.SemaphoreType.DMA((4,)),
        ],
        compiler_params=pltpu.CompilerParams(vmem_limit_bytes=VMEM_LIMIT),
        name="loss",
    )(
        meta,
        pattern,
        own_panel,
        *parts,
        loadings.reshape(blocks, 256, LANES),
        threshold.reshape(blocks, LANES),
        exposure.reshape(blocks, LANES),
        segment_map.reshape(blocks, LANES),
    )


def shifted(x, axis, k):
    n = lax.axis_size(axis)
    return lax.ppermute(x, axis, [(i, (i + k) % n) for i in range(n)])


def swapped(x, axis, k):
    return lax.ppermute(x, axis, [(i, i ^ k) for i in range(lax.axis_size(axis))])


def pair_sum(terms):
    while len(terms) > 1:
        terms = [terms[i] + terms[i + 1] for i in range(0, len(terms), 2)]
    return terms[0]


def body(
    generator,
    lattice_shift,
    loadings,
    load_pattern,
    threshold,
    exposure,
    segment_map,
    net_tiles,
    net_pattern,
):
    n_narrow = lax.axis_size("narrow")
    n_dest = lax.axis_size("wide")
    me = lax.axis_index("narrow")
    points = P_SIZE // n_narrow
    seg_blocks = net_tiles.shape[0]
    seg_dev = seg_blocks * LANES
    direct = n_dest <= 8

    own = jnp.stack([generator, lattice_shift])
    parts = [swapped(own, "narrow", k) for k in range(1, n_narrow)]
    quarter = [me ^ k for k in range(n_narrow)]
    base = lax.axis_index("wide") if direct else 0
    meta = jnp.stack([me * points, jnp.int32(base)] + quarter).astype(jnp.int32)

    vmem = pl.BlockSpec(memory_space=pltpu.VMEM)
    own_panel = pl.pallas_call(
        panel_kernel,
        out_shape=jax.ShapeDtypeStruct((2, own.shape[1] // LANES, points, LANES), jnp.bfloat16),
        in_specs=[pl.BlockSpec(memory_space=pltpu.SMEM), vmem],
        out_specs=vmem,
        name="panel",
    )(meta, own)
    pattern = load_pattern.reshape(-1)
    slots = net_tiles.shape[1]
    tiles = net_tiles.reshape(seg_blocks, slots * LANES, LANES)
    chunks = []
    first = 0
    for chunk in CHUNKS:
        chunk = chunk * points // sum(CHUNKS)
        partial = loss_call(
            meta,
            pattern,
            own_panel,
            parts,
            loadings,
            threshold,
            exposure,
            segment_map,
            n_dest,
            first,
            chunk,
            seg_dev,
            direct,
        )
        if direct:
            received = [partial[0]] + [shifted(partial[k], "wide", k) for k in range(1, n_dest)]
        else:
            received = [lax.all_to_all(partial[0], "wide", split_axis=0, concat_axis=0, tiled=True)]
        chunks.append((first, chunk, received))
        first += chunk
    done = None
    for first, chunk, received in chunks:
        done = net_call(net_pattern.reshape(-1), tiles, received, first, chunk, points, seg_dev, done)
    net_loss, sums = done

    total = pair_sum([sums] + [swapped(sums, "narrow", k) for k in range(1, n_narrow)])
    return (net_loss, total / P_SIZE)


def solution(mesh):
    return jax.shard_map(
        body,
        mesh=mesh,
        in_specs=(
            P("narrow"),
            P(("groups", "narrow")),
            P(("groups", "wide"), None, None, None),
            P(("groups", "wide"), None),
            P(("groups", "wide")),
            P(("groups", "wide")),
            P(("groups", "wide")),
            P(("groups", "wide"), None, None, None),
            P(("groups", "wide"), None),
        ),
        out_specs=(P("narrow", ("groups", "wide")), P(None, ("groups", "wide"))),
        check_vma=False,
    )
```

```python
import functools

import jax
import jax.numpy as jnp
from jax import lax
from jax.experimental import pallas as pl
from jax.experimental.pallas import tpu as pltpu
from jax.sharding import PartitionSpec as P

P_SIZE = 512
LANES = 128
ROWS = 16
DEST_CHUNK = 4
MXU = 256
CHUNKS = (64, 64)
VMEM_LIMIT = 63 << 20
NET_VMEM = 63 << 20

QUANTILE_MID = 2.6095163822174072
QUANTILE = (
    2.883376121520996,
    1.5978178977966309,
    0.023873422294855118,
    -0.0908193290233612,
    0.0662941262125969,
    -0.010339167900383472,
    -0.019267892464995384,
    0.011844170279800892,
    0.003007495542988181,
    -0.004063245374709368,
    -0.00016578214126639068,
    0.0005968576297163963,
)
CDF_SHIFT = 3.0
CDF_MID = 0.1666666716337204
CDF = (
    0.729083776473999,
    3.0559914112091064,
    8.280515670776367,
    10.208822250366211,
    -13.521076202392578,
    -54.16969680786133,
    43.550254821777344,
    285.4417419433594,
    -214.20135498046875,
    -1204.82958984375,
)
HALF_LOG2E = 0.7213475204444817


def horner(coefs, x):
    total = coefs[-1]
    for coef in coefs[-2::-1]:
        total = total * x + coef
    return total


def quantile(scaled):
    x = scaled.astype(jnp.float32) * (2.0**-31)
    s = 2.0 - jnp.log(1.0 - x * x)
    y = s * lax.rsqrt(s)
    return x * horner(QUANTILE, y - QUANTILE_MID)


def weighted_prob(t, exposure):
    y = jnp.abs(t)
    r = lax.rsqrt(y + CDF_SHIFT)
    q = r * r
    tail = jnp.exp2(t * t * -HALF_LOG2E) * q * horner(CDF, q - CDF_MID)
    return exposure * jnp.where(t > 0.0, 1.0 - tail, tail)


def fill_panel(panel, first, part, first_point):
    points = panel.shape[2]
    row = lax.broadcasted_iota(jnp.int32, (ROWS, LANES), 0) + first_point

    def fill(c, carry):
        at = pl.ds(pl.multiple_of(c * LANES, LANES), LANES)
        gen = part[0:1, at]
        shift = part[1:2, at]
        scaled = lax.shift_left(row * gen, 23) + (lax.shift_left(shift, 13) + (4096 - 2**31))
        jump = lax.shift_left(gen, 27)
        for r in range(points // ROWS):
            value = quantile(scaled).astype(jnp.bfloat16)
            rows = pl.ds(r * ROWS, ROWS)
            panel[0, first + c, rows, :] = value
            panel[1, first + c, rows, :] = pltpu.roll(value, LANES // 2, 1)
            scaled = scaled + jump
        return carry

    lax.fori_loop(0, part.shape[1] // LANES, fill, 0, unroll=max(1, 1024 // points))


def panel_kernel(part, panel):
    fill_panel(panel, 0, part, lax.axis_index("narrow") * panel.shape[2])


def loss_kernel(n_parts, n_dest, split, direct, first_point, pattern, *refs):
    me = lax.axis_index("narrow")
    base = lax.axis_index("wide") if direct else 0
    own_panel = refs[0]
    parts = refs[1:n_parts]
    sources = refs[n_parts : n_parts + 4]
    outs = refs[n_parts + 4 : -8]
    panel, load_ref, thr_ref, expo_ref, seg_ref, even, odd, sems = refs[-8:]
    masked = (even, odd)
    points = panel.shape[2]
    blocks = load_ref.shape[0]
    columns = own_panel.shape[1]
    all_points = own_panel.shape[2]
    seg_dev = (outs[0] if direct else outs[0].at[0]).shape[1]
    sub = seg_dev // (2 * MXU)
    group = split * sub
    steps = blocks // 2

    copies = [
        pltpu.make_async_copy(source, target, sems.at[i])
        for i, (source, target) in enumerate(zip(sources, (load_ref, thr_ref, expo_ref, seg_ref)))
    ]
    copies.append(
        pltpu.make_async_copy(
            own_panel.at[:, :, pl.ds(first_point, points), :],
            panel.at[:, pl.ds(me * columns, columns)],
            sems.at[4],
        )
    )
    for copy in copies:
        copy.start()

    for k in range(1, n_parts):
        fill_panel(panel, (me ^ k) * columns, parts[k - 1], me * all_points + first_point)

    for copy in copies:
        copy.wait()

    low = lax.broadcasted_iota(jnp.int32, (points, LANES), 1) < LANES // 2
    seg_row = lax.broadcasted_iota(jnp.int32, (ROWS, LANES), 0)

    def picked(b):
        halves = []
        for k in (0, 2):
            q0 = pattern[4 * b + k]
            q1 = pattern[4 * b + k + 1]
            left = panel[q0 & 1, lax.shift_right_logical(q0, 1)]
            right = panel[1 - (q1 & 1), lax.shift_right_logical(q1, 1)]
            halves.append(jnp.where(low, left, right))
        return jnp.concatenate(halves, axis=1)

    def one_pass(chunk, sums, latents):
        def project(step, parity):
            b = 2 * step
            loads = jnp.concatenate([load_ref[b], load_ref[b + 1]], axis=1)
            pltpu.matmul_push_rhs(loads, parity, parity)
            pltpu.matmul_acc_lhs(
                latents[parity], jnp.concatenate([picked(b), picked(b + 1)], axis=0), parity
            )

        def push_onehot(step, parity):
            local = [seg_ref[pl.ds(2 * step + j, 1), :] & (2 * MXU - 1) for j in range(2)]
            low_rows = [jnp.where(seg_row == (at & (ROWS - 1)), 1.0, 0.0).astype(jnp.bfloat16) for at in local]
            high = [
                jnp.broadcast_to(lax.shift_right_logical(at, 4), (ROWS, LANES)).astype(jnp.int16)
                for at in local
            ]
            for n in range(2):
                tile = [
                    jnp.concatenate(
                        [
                            jnp.where(high[j] == jnp.int16(n * MXU // ROWS + r), low_rows[j], jnp.bfloat16(0))
                            for r in range(MXU // ROWS)
                        ],
                        axis=0,
                    )
                    for j in range(2)
                ]
                pltpu.matmul_push_rhs(jnp.concatenate(tile, axis=1), parity, n, transpose=True)

        def add_up(parity):
            for n in range(2):
                pltpu.matmul_acc_lhs(sums[n], masked[parity][...], parity)

        def weigh(step, parity):
            latent = pltpu.matmul_pop(latents[parity])
            for j in range(2):
                one = pl.ds(2 * step + j, 1)
                here = slice(j * LANES, (j + 1) * LANES)
                t = thr_ref[one, :] - latent[j * points : (j + 1) * points, here]
                prob = weighted_prob(t, expo_ref[one, :]).astype(jnp.bfloat16)
                part = lax.shift_right_logical(seg_ref[one, :], (2 * MXU).bit_length() - 1) - base * sub
                part = jnp.where(part < 0, part + n_dest * sub, part) - chunk * group
                part = jnp.broadcast_to(part, (ROWS, LANES)).astype(jnp.int16)
                for d in range(group):
                    mine = part == jnp.int16(d)
                    for r in range(0, points, ROWS):
                        masked[parity][d * points + r : d * points + r + ROWS, here] = jnp.where(
                            mine, prob[r : r + ROWS], jnp.bfloat16(0)
                        )

        def stage(step, parity, ahead=True, behind=True):
            push_onehot(step, parity)
            if behind:
                add_up(1 - parity)
            if ahead:
                project(step + 1, 1 - parity)
            weigh(step, parity)

        project(0, 0)
        stage(0, 0, behind=False)

        def pair(i, carry):
            stage(2 * i + 1, 1)
            stage(2 * i + 2, 0)
            return carry

        lax.fori_loop(0, steps // 2 - 1, pair, 0)
        stage(steps - 1, 1, ahead=False)
        add_up(1)

        for n in range(2):
            total = pltpu.matmul_pop(sums[n])
            for d in range(split):
                for i in range(sub):
                    at = slice(i * 2 * MXU + n * MXU, i * 2 * MXU + (n + 1) * MXU)
                    value = total[(d * sub + i) * points : (d * sub + i + 1) * points]
                    if direct:
                        outs[d][:, at] = value.astype(outs[d].dtype)
                    else:
                        outs[0][chunk * split + d, :, at] = value.astype(jnp.bfloat16)

    def passes(*accs):
        if n_dest == split:
            one_pass(0, accs[:2], accs[2:])
        else:
            lax.fori_loop(0, n_dest // split, lambda c, x: (one_pass(c, accs[:2], accs[2:]), x)[1], 0)

    pl.run_scoped(
        passes,
        *[pltpu.ACC(n)((group * points, MXU), jnp.float32) for n in range(2)],
        *[pltpu.ACC(n)((2 * points, MXU), jnp.float32) for n in range(2)],
    )


def net_kernel(first_point, n_received, pattern, tiles_hbm, *refs):
    received = refs[:n_received]
    out_ref, sums_ref, losses, net_rows, tiles_ref, sem, sems = refs[-7:]
    before = refs[n_received : -7]
    blocks = tiles_ref.shape[0]
    copies = [pltpu.make_async_copy(tiles_hbm.at[b], tiles_ref.at[b], sems.at[b]) for b in range(blocks)]
    for copy in copies:
        copy.start()
    points = losses.shape[1]
    slots = tiles_ref.shape[1] // LANES
    for q in range(blocks):
        at = slice(q * LANES, (q + 1) * LANES)
        if n_received == 1:
            total = jnp.sum(received[0][:, :, at].astype(jnp.float32), axis=0)
        else:
            total = received[0][:, at].astype(jnp.float32)
            for ref in received[1:]:
                total = total + ref[:, at].astype(jnp.float32)
        losses[q] = total.astype(jnp.bfloat16)
    for b in range(blocks):
        at = slice(b * LANES, (b + 1) * LANES)
        picked = jnp.concatenate([losses[pattern[slots * b + k]] for k in range(slots)], axis=1)
        copies[b].wait()
        net = jnp.dot(picked, tiles_ref[b], preferred_element_type=jnp.float32)
        net_rows[:, at] = net
        first = jnp.sum(net, axis=0, keepdims=True)
        second = jnp.sum(net * net, axis=0, keepdims=True)
        if before:
            first += before[0][0:1, at]
            second += before[0][1:2, at]
        sums_ref[0:1, at] = first
        sums_ref[1:2, at] = second
    copy = pltpu.make_async_copy(net_rows, out_ref.at[pl.ds(first_point, points), :], sem)
    copy.start()
    copy.wait()


def net_call(net_pattern, tiles, received, first_point, chunk, points, seg_dev, before):
    vmem = pl.BlockSpec(memory_space=pltpu.VMEM)
    hbm = pl.BlockSpec(memory_space=pltpu.HBM)
    extra = [] if before is None else [before[1], before[0]]
    return pl.pallas_call(
        functools.partial(net_kernel, first_point, len(received)),
        out_shape=[
            jax.ShapeDtypeStruct((points, seg_dev), jnp.float32),
            jax.ShapeDtypeStruct((2, seg_dev), jnp.float32),
        ],
        in_specs=[pl.BlockSpec(memory_space=pltpu.SMEM)]
        + [hbm]
        + [vmem] * len(received)
        + [vmem, hbm][: len(extra)],
        out_specs=[hbm, vmem],
        scratch_shapes=[
            pltpu.VMEM((seg_dev // LANES, chunk, LANES), jnp.bfloat16),
            pltpu.VMEM((chunk, seg_dev), jnp.float32),
            pltpu.VMEM(tiles.shape, jnp.bfloat16),
            pltpu.SemaphoreType.DMA,
            pltpu.SemaphoreType.DMA((tiles.shape[0],)),
        ],
        input_output_aliases={} if before is None else {3 + len(received): 0},
        compiler_params=pltpu.CompilerParams(vmem_limit_bytes=NET_VMEM),
        name="net",
    )(net_pattern, tiles, *received, *extra)


def loss_call(pattern, own_panel, parts, loadings, threshold, exposure, segment_map, n_dest, first_point, points, seg_dev, direct):
    blocks = loadings.shape[0]
    n_parts = len(parts) + 1
    columns = own_panel.shape[1] * n_parts
    split = min(n_dest, DEST_CHUNK)
    if direct:
        out_shape = [
            jax.ShapeDtypeStruct((points, seg_dev), jnp.bfloat16 if d else jnp.float32)
            for d in range(n_dest)
        ]
    else:
        out_shape = [jax.ShapeDtypeStruct((n_dest, points, seg_dev), jnp.bfloat16)]
    slot = pltpu.VMEM((split * seg_dev // (2 * MXU) * points, MXU), jnp.bfloat16)
    vmem = pl.BlockSpec(memory_space=pltpu.VMEM)
    smem = pl.BlockSpec(memory_space=pltpu.SMEM)
    hbm = pl.BlockSpec(memory_space=pltpu.HBM)
    return pl.pallas_call(
        functools.partial(loss_kernel, n_parts, n_dest, split, direct, first_point),
        out_shape=out_shape,
        in_specs=[smem, hbm] + [vmem] * (n_parts - 1) + [hbm] * 4,
        out_specs=[vmem] * len(out_shape),
        scratch_shapes=[
            pltpu.VMEM((2, columns, points, LANES), jnp.bfloat16),
            pltpu.VMEM((blocks, 256, LANES), jnp.bfloat16),
            pltpu.VMEM((blocks, LANES), jnp.float32),
            pltpu.VMEM((blocks, LANES), jnp.float32),
            pltpu.VMEM((blocks, LANES), jnp.int32),
            slot,
            slot,
            pltpu.SemaphoreType.DMA((5,)),
        ],
        compiler_params=pltpu.CompilerParams(vmem_limit_bytes=VMEM_LIMIT),
        name="loss",
    )(
        pattern,
        own_panel,
        *parts,
        loadings.reshape(blocks, 256, LANES),
        threshold.reshape(blocks, LANES),
        exposure.reshape(blocks, LANES),
        segment_map.reshape(blocks, LANES),
    )


def shifted(x, axis, k):
    n = lax.axis_size(axis)
    return lax.ppermute(x, axis, [(i, (i + k) % n) for i in range(n)])


def swapped(x, axis, k):
    return lax.ppermute(x, axis, [(i, i ^ k) for i in range(lax.axis_size(axis))])


def pair_sum(terms):
    while len(terms) > 1:
        terms = [terms[i] + terms[i + 1] for i in range(0, len(terms), 2)]
    return terms[0]


def body(
    generator,
    lattice_shift,
    loadings,
    load_pattern,
    threshold,
    exposure,
    segment_map,
    net_tiles,
    net_pattern,
):
    n_narrow = lax.axis_size("narrow")
    n_dest = lax.axis_size("wide")
    points = P_SIZE // n_narrow
    seg_blocks = net_tiles.shape[0]
    seg_dev = seg_blocks * LANES
    direct = n_dest <= 8

    own = jnp.stack([generator, lattice_shift])
    parts = [swapped(own, "narrow", k) for k in range(1, n_narrow)]
    vmem = pl.BlockSpec(memory_space=pltpu.VMEM)
    own_panel = pl.pallas_call(
        panel_kernel,
        out_shape=jax.ShapeDtypeStruct((2, own.shape[1] // LANES, points, LANES), jnp.bfloat16),
        in_specs=[vmem],
        out_specs=vmem,
        name="panel",
    )(own)
    pattern = load_pattern.reshape(-1)
    slots = net_tiles.shape[1]
    tiles = net_tiles.reshape(seg_blocks, slots * LANES, LANES)
    chunks = []
    first = 0
    for chunk in CHUNKS:
        chunk = chunk * points // sum(CHUNKS)
        partial = loss_call(
            pattern,
            own_panel,
            parts,
            loadings,
            threshold,
            exposure,
            segment_map,
            n_dest,
            first,
            chunk,
            seg_dev,
            direct,
        )
        if direct:
            received = [partial[0]] + [shifted(partial[k], "wide", k) for k in range(1, n_dest)]
        else:
            received = [lax.all_to_all(partial[0], "wide", split_axis=0, concat_axis=0, tiled=True)]
        chunks.append((first, chunk, received))
        first += chunk
    done = None
    for first, chunk, received in chunks:
        done = net_call(net_pattern.reshape(-1), tiles, received, first, chunk, points, seg_dev, done)
    net_loss, sums = done

    total = pair_sum([sums] + [swapped(sums, "narrow", k) for k in range(1, n_narrow)])
    return (net_loss, total / P_SIZE)


def solution(mesh):
    return jax.shard_map(
        body,
        mesh=mesh,
        in_specs=(
            P("narrow"),
            P(("groups", "narrow")),
            P(("groups", "wide"), None, None, None),
            P(("groups", "wide"), None),
            P(("groups", "wide")),
            P(("groups", "wide")),
            P(("groups", "wide")),
            P(("groups", "wide"), None, None, None),
            P(("groups", "wide"), None),
        ),
        out_specs=(P("narrow", ("groups", "wide")), P(None, ("groups", "wide"))),
        check_vma=False,
    )
```

```python
import functools

import jax
import jax.numpy as jnp
from jax import lax
from jax.experimental import pallas as pl
from jax.experimental.pallas import tpu as pltpu
from jax.sharding import PartitionSpec as P

P_SIZE = 512
LANES = 128
ROWS = 16
DEST_CHUNK = 4
MXU = 256
CHUNKS = (64, 64)
VMEM_LIMIT = 63 << 20
NET_VMEM = 16 << 20

QUANTILE_MID = 2.6095163822174072
QUANTILE = (
    2.883376121520996,
    1.5978178977966309,
    0.023873422294855118,
    -0.0908193290233612,
    0.0662941262125969,
    -0.010339167900383472,
    -0.019267892464995384,
    0.011844170279800892,
    0.003007495542988181,
    -0.004063245374709368,
    -0.00016578214126639068,
    0.0005968576297163963,
)
CDF_SHIFT = 3.0
CDF_MID = 0.1666666716337204
CDF = (
    0.729083776473999,
    3.0559914112091064,
    8.280515670776367,
    10.208822250366211,
    -13.521076202392578,
    -54.16969680786133,
    43.550254821777344,
    285.4417419433594,
    -214.20135498046875,
    -1204.82958984375,
)
HALF_LOG2E = 0.7213475204444817


def horner(coefs, x):
    total = coefs[-1]
    for coef in coefs[-2::-1]:
        total = total * x + coef
    return total


def quantile(scaled):
    x = scaled.astype(jnp.float32) * (2.0**-31)
    s = 2.0 - jnp.log(1.0 - x * x)
    y = s * lax.rsqrt(s)
    return x * horner(QUANTILE, y - QUANTILE_MID)


def weighted_prob(t, exposure):
    y = jnp.abs(t)
    r = lax.rsqrt(y + CDF_SHIFT)
    q = r * r
    tail = jnp.exp2(t * t * -HALF_LOG2E) * q * horner(CDF, q - CDF_MID)
    return exposure * jnp.where(t > 0.0, 1.0 - tail, tail)


def fill_panel(panel, first, part, first_point):
    points = panel.shape[2]
    row = lax.broadcasted_iota(jnp.int32, (ROWS, LANES), 0) + first_point

    def fill(c, carry):
        at = pl.ds(pl.multiple_of(c * LANES, LANES), LANES)
        gen = part[0:1, at]
        shift = part[1:2, at]
        scaled = lax.shift_left(row * gen, 23) + (lax.shift_left(shift, 13) + (4096 - 2**31))
        jump = lax.shift_left(gen, 27)
        for r in range(points // ROWS):
            value = quantile(scaled).astype(jnp.bfloat16)
            rows = pl.ds(r * ROWS, ROWS)
            panel[0, first + c, rows, :] = value
            panel[1, first + c, rows, :] = pltpu.roll(value, LANES // 2, 1)
            scaled = scaled + jump
        return carry

    lax.fori_loop(0, part.shape[1] // LANES, fill, 0, unroll=part.shape[1] // LANES)


def panel_kernel(part, panel):
    fill_panel(panel, 0, part, lax.axis_index("narrow") * panel.shape[2])


def loss_kernel(n_parts, n_dest, split, direct, first_point, pattern, *refs):
    me = lax.axis_index("narrow")
    base = lax.axis_index("wide") if direct else 0
    own_panel = refs[0]
    parts = refs[1:n_parts]
    sources = refs[n_parts : n_parts + 4]
    outs = refs[n_parts + 4 : -8]
    panel, load_ref, thr_ref, expo_ref, seg_ref, even, odd, sems = refs[-8:]
    masked = (even, odd)
    points = panel.shape[2]
    blocks = load_ref.shape[0]
    columns = own_panel.shape[1]
    all_points = own_panel.shape[2]
    seg_dev = (outs[0] if direct else outs[0].at[0]).shape[1]
    sub = seg_dev // (2 * MXU)
    group = split * sub
    steps = blocks // 2

    copies = [
        pltpu.make_async_copy(source, target, sems.at[i])
        for i, (source, target) in enumerate(zip(sources, (load_ref, thr_ref, expo_ref, seg_ref)))
    ]
    copies.append(
        pltpu.make_async_copy(
            own_panel.at[:, :, pl.ds(first_point, points), :],
            panel.at[:, pl.ds(me * columns, columns)],
            sems.at[4],
        )
    )
    for copy in copies:
        copy.start()

    for k in range(1, n_parts):
        fill_panel(panel, (me ^ k) * columns, parts[k - 1], me * all_points + first_point)

    for copy in copies:
        copy.wait()

    low = lax.broadcasted_iota(jnp.int32, (points, LANES), 1) < LANES // 2
    seg_row = lax.broadcasted_iota(jnp.int32, (ROWS, LANES), 0)

    def picked(b):
        halves = []
        for k in (0, 2):
            q0 = pattern[k, b]
            q1 = pattern[k + 1, b]
            left = panel[q0 & 1, lax.shift_right_logical(q0, 1)]
            right = panel[1 - (q1 & 1), lax.shift_right_logical(q1, 1)]
            halves.append(jnp.where(low, left, right))
        return jnp.concatenate(halves, axis=1)

    def one_pass(chunk, sums, latents):
        def project(step, parity):
            b = 2 * step
            loads = jnp.concatenate([load_ref[b], load_ref[b + 1]], axis=1)
            pltpu.matmul_push_rhs(loads, parity, parity)
            pltpu.matmul_acc_lhs(
                latents[parity], jnp.concatenate([picked(b), picked(b + 1)], axis=0), parity
            )

        def push_onehot(step, parity):
            local = [seg_ref[pl.ds(2 * step + j, 1), :] & (2 * MXU - 1) for j in range(2)]
            low_rows = [jnp.where(seg_row == (at & (ROWS - 1)), 1.0, 0.0).astype(jnp.bfloat16) for at in local]
            high = [
                jnp.broadcast_to(lax.shift_right_logical(at, 4), (ROWS, LANES)).astype(jnp.int16)
                for at in local
            ]
            for n in range(2):
                tile = [
                    jnp.concatenate(
                        [
                            jnp.where(high[j] == jnp.int16(n * MXU // ROWS + r), low_rows[j], jnp.bfloat16(0))
                            for r in range(MXU // ROWS)
                        ],
                        axis=0,
                    )
                    for j in range(2)
                ]
                pltpu.matmul_push_rhs(jnp.concatenate(tile, axis=1), parity, n, transpose=True)

        def add_up(parity):
            for n in range(2):
                pltpu.matmul_acc_lhs(sums[n], masked[parity][...], parity)

        def weigh(step, parity):
            latent = pltpu.matmul_pop(latents[parity])
            for j in range(2):
                one = pl.ds(2 * step + j, 1)
                here = slice(j * LANES, (j + 1) * LANES)
                t = thr_ref[one, :] - latent[j * points : (j + 1) * points, here]
                prob = weighted_prob(t, expo_ref[one, :]).astype(jnp.bfloat16)
                part = lax.shift_right_logical(seg_ref[one, :], (2 * MXU).bit_length() - 1) - base * sub
                part = jnp.where(part < 0, part + n_dest * sub, part) - chunk * group
                part = jnp.broadcast_to(part, (ROWS, LANES)).astype(jnp.int16)
                for d in range(group):
                    mine = part == jnp.int16(d)
                    for r in range(0, points, ROWS):
                        masked[parity][d * points + r : d * points + r + ROWS, here] = jnp.where(
                            mine, prob[r : r + ROWS], jnp.bfloat16(0)
                        )

        def stage(step, parity, ahead=True, behind=True):
            push_onehot(step, parity)
            if behind:
                add_up(1 - parity)
            if ahead:
                project(step + 1, 1 - parity)
            weigh(step, parity)

        project(0, 0)
        stage(0, 0, behind=False)

        def pair(i, carry):
            stage(2 * i + 1, 1)
            stage(2 * i + 2, 0)
            return carry

        lax.fori_loop(0, steps // 2 - 1, pair, 0)
        stage(steps - 1, 1, ahead=False)
        add_up(1)

        for n in range(2):
            total = pltpu.matmul_pop(sums[n])
            for d in range(split):
                for i in range(sub):
                    at = slice(i * 2 * MXU + n * MXU, i * 2 * MXU + (n + 1) * MXU)
                    value = total[(d * sub + i) * points : (d * sub + i + 1) * points]
                    if direct:
                        outs[d][:, at] = value.astype(outs[d].dtype)
                    else:
                        outs[0][chunk * split + d, :, at] = value.astype(jnp.bfloat16)

    def passes(*accs):
        if n_dest == split:
            one_pass(0, accs[:2], accs[2:])
        else:
            lax.fori_loop(0, n_dest // split, lambda c, x: (one_pass(c, accs[:2], accs[2:]), x)[1], 0)

    pl.run_scoped(
        passes,
        *[pltpu.ACC(n)((group * points, MXU), jnp.float32) for n in range(2)],
        *[pltpu.ACC(n)((2 * points, MXU), jnp.float32) for n in range(2)],
    )


def net_kernel(first_point, n_received, pattern, tiles_ref, *refs):
    received = refs[:n_received]
    out_ref, sums_ref, losses, net_rows, sem = refs[-5:]
    before = refs[n_received : -5]
    blocks = tiles_ref.shape[0]
    points = losses.shape[1]
    slots = tiles_ref.shape[1] // LANES
    for q in range(blocks):
        at = slice(q * LANES, (q + 1) * LANES)
        if n_received == 1:
            total = jnp.sum(received[0][:, :, at].astype(jnp.float32), axis=0)
        else:
            total = received[0][:, at].astype(jnp.float32)
            for ref in received[1:]:
                total = total + ref[:, at].astype(jnp.float32)
        losses[q] = total.astype(jnp.bfloat16)
    for b in range(blocks):
        at = slice(b * LANES, (b + 1) * LANES)
        picked = jnp.concatenate([losses[pattern[b, k]] for k in range(slots)], axis=1)
        net = jnp.dot(picked, tiles_ref[b], preferred_element_type=jnp.float32)
        net_rows[:, at] = net
        first = jnp.sum(net, axis=0, keepdims=True)
        second = jnp.sum(net * net, axis=0, keepdims=True)
        if before:
            first += before[0][0:1, at]
            second += before[0][1:2, at]
        sums_ref[0:1, at] = first
        sums_ref[1:2, at] = second
    copy = pltpu.make_async_copy(net_rows, out_ref.at[pl.ds(first_point, points), :], sem)
    copy.start()
    copy.wait()


def net_call(net_pattern, tiles, received, first_point, chunk, points, seg_dev, before):
    vmem = pl.BlockSpec(memory_space=pltpu.VMEM)
    hbm = pl.BlockSpec(memory_space=pltpu.HBM)
    extra = [] if before is None else [before[1], before[0]]
    return pl.pallas_call(
        functools.partial(net_kernel, first_point, len(received)),
        out_shape=[
            jax.ShapeDtypeStruct((points, seg_dev), jnp.float32),
            jax.ShapeDtypeStruct((2, seg_dev), jnp.float32),
        ],
        in_specs=[pl.BlockSpec(memory_space=pltpu.SMEM)]
        + [vmem] * (1 + len(received))
        + [vmem, hbm][: len(extra)],
        out_specs=[hbm, vmem],
        scratch_shapes=[
            pltpu.VMEM((seg_dev // LANES, chunk, LANES), jnp.bfloat16),
            pltpu.VMEM((chunk, seg_dev), jnp.float32),
            pltpu.SemaphoreType.DMA,
        ],
        input_output_aliases={} if before is None else {3 + len(received): 0},
        compiler_params=pltpu.CompilerParams(vmem_limit_bytes=NET_VMEM),
        name="net",
    )(net_pattern, tiles, *received, *extra)


def loss_call(pattern, own_panel, parts, loadings, threshold, exposure, segment_map, n_dest, first_point, points, seg_dev, direct):
    blocks = loadings.shape[0]
    n_parts = len(parts) + 1
    columns = own_panel.shape[1] * n_parts
    split = min(n_dest, DEST_CHUNK)
    if direct:
        out_shape = [
            jax.ShapeDtypeStruct((points, seg_dev), jnp.bfloat16 if d else jnp.float32)
            for d in range(n_dest)
        ]
    else:
        out_shape = [jax.ShapeDtypeStruct((n_dest, points, seg_dev), jnp.bfloat16)]
    slot = pltpu.VMEM((split * seg_dev // (2 * MXU) * points, MXU), jnp.bfloat16)
    vmem = pl.BlockSpec(memory_space=pltpu.VMEM)
    smem = pl.BlockSpec(memory_space=pltpu.SMEM)
    hbm = pl.BlockSpec(memory_space=pltpu.HBM)
    return pl.pallas_call(
        functools.partial(loss_kernel, n_parts, n_dest, split, direct, first_point),
        out_shape=out_shape,
        in_specs=[smem, hbm] + [vmem] * (n_parts - 1) + [hbm] * 4,
        out_specs=[vmem] * len(out_shape),
        scratch_shapes=[
            pltpu.VMEM((2, columns, points, LANES), jnp.bfloat16),
            pltpu.VMEM((blocks, 256, LANES), jnp.bfloat16),
            pltpu.VMEM((blocks, LANES), jnp.float32),
            pltpu.VMEM((blocks, LANES), jnp.float32),
            pltpu.VMEM((blocks, LANES), jnp.int32),
            slot,
            slot,
            pltpu.SemaphoreType.DMA((5,)),
        ],
        compiler_params=pltpu.CompilerParams(vmem_limit_bytes=VMEM_LIMIT),
        name="loss",
    )(
        pattern,
        own_panel,
        *parts,
        loadings.reshape(blocks, 256, LANES),
        threshold.reshape(blocks, LANES),
        exposure.reshape(blocks, LANES),
        segment_map.reshape(blocks, LANES),
    )


def shifted(x, axis, k):
    n = lax.axis_size(axis)
    return lax.ppermute(x, axis, [(i, (i + k) % n) for i in range(n)])


def swapped(x, axis, k):
    return lax.ppermute(x, axis, [(i, i ^ k) for i in range(lax.axis_size(axis))])


def pair_sum(terms):
    while len(terms) > 1:
        terms = [terms[i] + terms[i + 1] for i in range(0, len(terms), 2)]
    return terms[0]


def body(
    generator,
    lattice_shift,
    loadings,
    load_pattern,
    threshold,
    exposure,
    segment_map,
    net_tiles,
    net_pattern,
):
    n_narrow = lax.axis_size("narrow")
    n_dest = lax.axis_size("wide")
    points = P_SIZE // n_narrow
    seg_blocks = net_tiles.shape[0]
    seg_dev = seg_blocks * LANES
    direct = n_dest <= 8

    own = jnp.stack([generator, lattice_shift])
    parts = [swapped(own, "narrow", k) for k in range(1, n_narrow)]
    vmem = pl.BlockSpec(memory_space=pltpu.VMEM)
    own_panel = pl.pallas_call(
        panel_kernel,
        out_shape=jax.ShapeDtypeStruct((2, own.shape[1] // LANES, points, LANES), jnp.bfloat16),
        in_specs=[vmem],
        out_specs=vmem,
        name="panel",
    )(own)
    pattern = load_pattern.T
    slots = net_tiles.shape[1]
    tiles = net_tiles.reshape(seg_blocks, slots * LANES, LANES)
    chunks = []
    first = 0
    for chunk in CHUNKS:
        chunk = chunk * points // sum(CHUNKS)
        partial = loss_call(
            pattern,
            own_panel,
            parts,
            loadings,
            threshold,
            exposure,
            segment_map,
            n_dest,
            first,
            chunk,
            seg_dev,
            direct,
        )
        if direct:
            received = [partial[0]] + [shifted(partial[k], "wide", k) for k in range(1, n_dest)]
        else:
            received = [lax.all_to_all(partial[0], "wide", split_axis=0, concat_axis=0, tiled=True)]
        chunks.append((first, chunk, received))
        first += chunk
    done = None
    for first, chunk, received in chunks:
        done = net_call(net_pattern, tiles, received, first, chunk, points, seg_dev, done)
    net_loss, sums = done

    total = pair_sum([sums] + [swapped(sums, "narrow", k) for k in range(1, n_narrow)])
    return (net_loss, total / P_SIZE)


def solution(mesh):
    return jax.shard_map(
        body,
        mesh=mesh,
        in_specs=(
            P("narrow"),
            P(("groups", "narrow")),
            P(("groups", "wide"), None, None, None),
            P(("groups", "wide"), None),
            P(("groups", "wide")),
            P(("groups", "wide")),
            P(("groups", "wide")),
            P(("groups", "wide"), None, None, None),
            P(("groups", "wide"), None),
        ),
        out_specs=(P("narrow", ("groups", "wide")), P(None, ("groups", "wide"))),
        check_vma=False,
    )
```

```python
import functools

import jax
import jax.numpy as jnp
from jax import lax
from jax.experimental import pallas as pl
from jax.experimental.pallas import tpu as pltpu
from jax.sharding import PartitionSpec as P

P_SIZE = 512
LANES = 128
ROWS = 16
DEST_CHUNK = 4
MXU = 256
CHUNKS = (80, 48)
VMEM_LIMIT = 63 << 20
NET_VMEM = 16 << 20

QUANTILE_MID = 2.6095163822174072
QUANTILE = (
    2.883376121520996,
    1.5978178977966309,
    0.023873422294855118,
    -0.0908193290233612,
    0.0662941262125969,
    -0.010339167900383472,
    -0.019267892464995384,
    0.011844170279800892,
    0.003007495542988181,
    -0.004063245374709368,
    -0.00016578214126639068,
    0.0005968576297163963,
)
CDF_SHIFT = 3.0
CDF_MID = 0.1666666716337204
CDF = (
    0.729083776473999,
    3.0559914112091064,
    8.280515670776367,
    10.208822250366211,
    -13.521076202392578,
    -54.16969680786133,
    43.550254821777344,
    285.4417419433594,
    -214.20135498046875,
    -1204.82958984375,
)
HALF_LOG2E = 0.7213475204444817


def horner(coefs, x):
    total = coefs[-1]
    for coef in coefs[-2::-1]:
        total = total * x + coef
    return total


def quantile(scaled):
    x = scaled.astype(jnp.float32) * (2.0**-31)
    s = 2.0 - jnp.log(1.0 - x * x)
    y = s * lax.rsqrt(s)
    return x * horner(QUANTILE, y - QUANTILE_MID)


def weighted_prob(t, exposure):
    y = jnp.abs(t)
    r = lax.rsqrt(y + CDF_SHIFT)
    q = r * r
    tail = jnp.exp2(t * t * -HALF_LOG2E) * q * horner(CDF, q - CDF_MID)
    return exposure * jnp.where(t > 0.0, 1.0 - tail, tail)


def fill_panel(panel, first, part, first_point):
    points = panel.shape[2]
    row = lax.broadcasted_iota(jnp.int32, (ROWS, LANES), 0) + first_point

    def fill(c, carry):
        at = pl.ds(pl.multiple_of(c * LANES, LANES), LANES)
        gen = part[0:1, at]
        shift = part[1:2, at]
        scaled = lax.shift_left(row * gen, 23) + (lax.shift_left(shift, 13) + (4096 - 2**31))
        jump = lax.shift_left(gen, 27)
        for r in range(points // ROWS):
            value = quantile(scaled).astype(jnp.bfloat16)
            rows = pl.ds(r * ROWS, ROWS)
            panel[0, first + c, rows, :] = value
            panel[1, first + c, rows, :] = pltpu.roll(value, LANES // 2, 1)
            scaled = scaled + jump
        return carry

    lax.fori_loop(0, part.shape[1] // LANES, fill, 0, unroll=part.shape[1] // LANES)


def panel_kernel(all_points, part, panel):
    fill_panel(panel, 0, part, lax.axis_index("narrow") * all_points)


def loss_kernel(n_parts, n_dest, split, direct, has_panel, all_points, first_point, pattern, *refs):
    me = lax.axis_index("narrow")
    base = lax.axis_index("wide") if direct else 0
    parts = refs[:n_parts]
    sources = refs[n_parts : n_parts + 4]
    outs = refs[n_parts + 4 : -8]
    panel, load_ref, thr_ref, expo_ref, seg_ref, even, odd, sems = refs[-8:]
    masked = (even, odd)
    points = panel.shape[2]
    blocks = load_ref.shape[0]
    columns = parts[-1].shape[1] // LANES
    seg_dev = (outs[0] if direct else outs[0].at[0]).shape[1]
    sub = seg_dev // (2 * MXU)
    group = split * sub
    steps = blocks // 2

    copies = [
        pltpu.make_async_copy(source, target, sems.at[i])
        for i, (source, target) in enumerate(zip(sources, (load_ref, thr_ref, expo_ref, seg_ref)))
    ]
    if has_panel:
        copies.append(
            pltpu.make_async_copy(parts[0], panel.at[:, pl.ds(me * columns, columns)], sems.at[4])
        )
    for copy in copies:
        copy.start()

    for k in range(int(has_panel), n_parts):
        fill_panel(panel, (me ^ k) * columns, parts[k], me * all_points + first_point)

    for copy in copies:
        copy.wait()

    low = lax.broadcasted_iota(jnp.int32, (points, LANES), 1) < LANES // 2
    seg_row = lax.broadcasted_iota(jnp.int32, (ROWS, LANES), 0)

    def picked(b):
        halves = []
        for k in (0, 2):
            q0 = pattern[k, b]
            q1 = pattern[k + 1, b]
            left = panel[q0 & 1, lax.shift_right_logical(q0, 1)]
            right = panel[1 - (q1 & 1), lax.shift_right_logical(q1, 1)]
            halves.append(jnp.where(low, left, right))
        return jnp.concatenate(halves, axis=1)

    def one_pass(chunk, sums, latents):
        def project(step, parity):
            b = 2 * step
            loads = jnp.concatenate([load_ref[b], load_ref[b + 1]], axis=1)
            pltpu.matmul_push_rhs(loads, parity, parity)
            pltpu.matmul_acc_lhs(
                latents[parity], jnp.concatenate([picked(b), picked(b + 1)], axis=0), parity
            )

        def push_onehot(step, parity):
            local = [seg_ref[pl.ds(2 * step + j, 1), :] & (2 * MXU - 1) for j in range(2)]
            low_rows = [jnp.where(seg_row == (at & (ROWS - 1)), 1.0, 0.0).astype(jnp.bfloat16) for at in local]
            high = [
                jnp.broadcast_to(lax.shift_right_logical(at, 4), (ROWS, LANES)).astype(jnp.int16)
                for at in local
            ]
            for n in range(2):
                tile = [
                    jnp.concatenate(
                        [
                            jnp.where(high[j] == jnp.int16(n * MXU // ROWS + r), low_rows[j], jnp.bfloat16(0))
                            for r in range(MXU // ROWS)
                        ],
                        axis=0,
                    )
                    for j in range(2)
                ]
                pltpu.matmul_push_rhs(jnp.concatenate(tile, axis=1), parity, n, transpose=True)

        def add_up(parity):
            for n in range(2):
                pltpu.matmul_acc_lhs(sums[n], masked[parity][...], parity)

        def weigh(step, parity):
            latent = pltpu.matmul_pop(latents[parity])
            for j in range(2):
                one = pl.ds(2 * step + j, 1)
                here = slice(j * LANES, (j + 1) * LANES)
                t = thr_ref[one, :] - latent[j * points : (j + 1) * points, here]
                prob = weighted_prob(t, expo_ref[one, :]).astype(jnp.bfloat16)
                part = lax.shift_right_logical(seg_ref[one, :], (2 * MXU).bit_length() - 1) - base * sub
                part = jnp.where(part < 0, part + n_dest * sub, part) - chunk * group
                part = jnp.broadcast_to(part, (ROWS, LANES)).astype(jnp.int16)
                for d in range(group):
                    mine = part == jnp.int16(d)
                    for r in range(0, points, ROWS):
                        masked[parity][d * points + r : d * points + r + ROWS, here] = jnp.where(
                            mine, prob[r : r + ROWS], jnp.bfloat16(0)
                        )

        def stage(step, parity, ahead=True, behind=True):
            push_onehot(step, parity)
            if behind:
                add_up(1 - parity)
            if ahead:
                project(step + 1, 1 - parity)
            weigh(step, parity)

        project(0, 0)
        stage(0, 0, behind=False)

        def pair(i, carry):
            stage(2 * i + 1, 1)
            stage(2 * i + 2, 0)
            return carry

        lax.fori_loop(0, steps // 2 - 1, pair, 0)
        stage(steps - 1, 1, ahead=False)
        add_up(1)

        for n in range(2):
            total = pltpu.matmul_pop(sums[n])
            for d in range(split):
                for i in range(sub):
                    at = slice(i * 2 * MXU + n * MXU, i * 2 * MXU + (n + 1) * MXU)
                    value = total[(d * sub + i) * points : (d * sub + i + 1) * points]
                    if direct:
                        outs[d][:, at] = value.astype(outs[d].dtype)
                    else:
                        outs[0][chunk * split + d, :, at] = value.astype(jnp.bfloat16)

    def passes(*accs):
        if n_dest == split:
            one_pass(0, accs[:2], accs[2:])
        else:
            lax.fori_loop(0, n_dest // split, lambda c, x: (one_pass(c, accs[:2], accs[2:]), x)[1], 0)

    pl.run_scoped(
        passes,
        *[pltpu.ACC(n)((group * points, MXU), jnp.float32) for n in range(2)],
        *[pltpu.ACC(n)((2 * points, MXU), jnp.float32) for n in range(2)],
    )


def net_kernel(first_point, n_received, has_before, pattern, tiles_ref, *refs):
    received = refs[:n_received]
    losses, net_rows, sem, keep_sem = refs[-4:]
    n_before = 2 if has_before else 0
    before = refs[n_received : n_received + n_before]
    keep = refs[n_received + n_before : -4]
    if len(keep) == 4:
        keep_in, out_ref, sums_ref, keep_out = keep
        keep_copy = pltpu.make_async_copy(keep_in, keep_out, keep_sem)
        keep_copy.start()
    else:
        keep_copy = None
        out_ref, sums_ref = keep
    blocks = tiles_ref.shape[0]
    points = losses.shape[1]
    slots = tiles_ref.shape[1] // LANES
    for q in range(blocks):
        at = slice(q * LANES, (q + 1) * LANES)
        if n_received == 1:
            total = jnp.sum(received[0][:, :, at].astype(jnp.float32), axis=0)
        else:
            total = received[0][:, at].astype(jnp.float32)
            for ref in received[1:]:
                total = total + ref[:, at].astype(jnp.float32)
        losses[q] = total.astype(jnp.bfloat16)
    for b in range(blocks):
        at = slice(b * LANES, (b + 1) * LANES)
        picked = jnp.concatenate([losses[pattern[b, k]] for k in range(slots)], axis=1)
        net = jnp.dot(picked, tiles_ref[b], preferred_element_type=jnp.float32)
        net_rows[:, at] = net
        first = jnp.sum(net, axis=0, keepdims=True)
        second = jnp.sum(net * net, axis=0, keepdims=True)
        if before:
            first += before[0][0:1, at]
            second += before[0][1:2, at]
        sums_ref[0:1, at] = first
        sums_ref[1:2, at] = second
    copy = pltpu.make_async_copy(net_rows, out_ref.at[pl.ds(first_point, points), :], sem)
    copy.start()
    copy.wait()
    if keep_copy is not None:
        keep_copy.wait()


def net_call(net_pattern, tiles, received, first_point, chunk, points, seg_dev, before, keep):
    vmem = pl.BlockSpec(memory_space=pltpu.VMEM)
    hbm = pl.BlockSpec(memory_space=pltpu.HBM)
    extra = [] if before is None else [before[1], before[0]]
    return pl.pallas_call(
        functools.partial(net_kernel, first_point, len(received), before is not None),
        out_shape=[
            jax.ShapeDtypeStruct((points, seg_dev), jnp.float32),
            jax.ShapeDtypeStruct((2, seg_dev), jnp.float32),
        ]
        + [jax.ShapeDtypeStruct(k.shape, k.dtype) for k in keep],
        in_specs=[pl.BlockSpec(memory_space=pltpu.SMEM)]
        + [vmem] * (1 + len(received))
        + [vmem, hbm][: len(extra)]
        + [hbm] * len(keep),
        out_specs=[hbm, vmem] + [vmem] * len(keep),
        scratch_shapes=[
            pltpu.VMEM((seg_dev // LANES, chunk, LANES), jnp.bfloat16),
            pltpu.VMEM((chunk, seg_dev), jnp.float32),
            pltpu.SemaphoreType.DMA,
            pltpu.SemaphoreType.DMA,
        ],
        input_output_aliases={} if before is None else {3 + len(received): 0},
        compiler_params=pltpu.CompilerParams(vmem_limit_bytes=NET_VMEM),
        name="net",
    )(net_pattern, tiles, *received, *extra, *keep)


def loss_call(pattern, parts, has_panel, loadings, threshold, exposure, segment_map, n_dest, all_points, first_point, points, seg_dev, direct):
    blocks = loadings.shape[0]
    n_parts = len(parts)
    columns = parts[-1].shape[1] // LANES * n_parts
    split = min(n_dest, DEST_CHUNK)
    if direct:
        out_shape = [
            jax.ShapeDtypeStruct((points, seg_dev), jnp.bfloat16 if d else jnp.float32)
            for d in range(n_dest)
        ]
    else:
        out_shape = [jax.ShapeDtypeStruct((n_dest, points, seg_dev), jnp.bfloat16)]
    slot = pltpu.VMEM((split * seg_dev // (2 * MXU) * points, MXU), jnp.bfloat16)
    vmem = pl.BlockSpec(memory_space=pltpu.VMEM)
    smem = pl.BlockSpec(memory_space=pltpu.SMEM)
    hbm = pl.BlockSpec(memory_space=pltpu.HBM)
    return pl.pallas_call(
        functools.partial(loss_kernel, n_parts, n_dest, split, direct, has_panel, all_points, first_point),
        out_shape=out_shape,
        in_specs=[smem, hbm if has_panel else vmem] + [vmem] * (n_parts - 1) + [hbm] * 4,
        out_specs=[vmem] * len(out_shape),
        scratch_shapes=[
            pltpu.VMEM((2, columns, points, LANES), jnp.bfloat16),
            pltpu.VMEM((blocks, 256, LANES), jnp.bfloat16),
            pltpu.VMEM((blocks, LANES), jnp.float32),
            pltpu.VMEM((blocks, LANES), jnp.float32),
            pltpu.VMEM((blocks, LANES), jnp.int32),
            slot,
            slot,
            pltpu.SemaphoreType.DMA((5,)),
        ],
        compiler_params=pltpu.CompilerParams(vmem_limit_bytes=VMEM_LIMIT),
        name="loss",
    )(
        pattern,
        *parts,
        loadings.reshape(blocks, 256, LANES),
        threshold.reshape(blocks, LANES),
        exposure.reshape(blocks, LANES),
        segment_map.reshape(blocks, LANES),
    )


def shifted(x, axis, k):
    n = lax.axis_size(axis)
    return lax.ppermute(x, axis, [(i, (i + k) % n) for i in range(n)])


def swapped(x, axis, k):
    return lax.ppermute(x, axis, [(i, i ^ k) for i in range(lax.axis_size(axis))])


def pair_sum(terms):
    while len(terms) > 1:
        terms = [terms[i] + terms[i + 1] for i in range(0, len(terms), 2)]
    return terms[0]


def body(
    generator,
    lattice_shift,
    loadings,
    load_pattern,
    threshold,
    exposure,
    segment_map,
    net_tiles,
    net_pattern,
):
    n_narrow = lax.axis_size("narrow")
    n_dest = lax.axis_size("wide")
    points = P_SIZE // n_narrow
    seg_blocks = net_tiles.shape[0]
    seg_dev = seg_blocks * LANES
    direct = n_dest <= 8

    own = jnp.stack([generator, lattice_shift])
    parts = [swapped(own, "narrow", k) for k in range(1, n_narrow)]
    vmem = pl.BlockSpec(memory_space=pltpu.VMEM)
    own_panel = pl.pallas_call(
        functools.partial(panel_kernel, points),
        out_shape=jax.ShapeDtypeStruct(
            (2, own.shape[1] // LANES, CHUNKS[0] * points // sum(CHUNKS), LANES), jnp.bfloat16
        ),
        in_specs=[vmem],
        out_specs=vmem,
        name="panel",
    )(own)
    pattern = load_pattern.T
    slots = net_tiles.shape[1]
    tiles = net_tiles.reshape(seg_blocks, slots * LANES, LANES)
    chunks = []
    first = 0
    for chunk in CHUNKS:
        chunk = chunk * points // sum(CHUNKS)
        partial = loss_call(
            pattern,
            [own_panel if first == 0 else own] + parts,
            first == 0,
            loadings,
            threshold,
            exposure,
            segment_map,
            n_dest,
            points,
            first,
            chunk,
            seg_dev,
            direct,
        )
        if direct:
            received = [partial[0]] + [shifted(partial[k], "wide", k) for k in range(1, n_dest)]
        else:
            received = [lax.all_to_all(partial[0], "wide", split_axis=0, concat_axis=0, tiled=True)]
        chunks.append((first, chunk, received))
        first += chunk
    done = None
    for i, (first, chunk, received) in enumerate(chunks):
        keep = [chunks[i + 1][2][0]] if direct and i + 1 < len(chunks) else []
        *done, = net_call(net_pattern, tiles, received, first, chunk, points, seg_dev, done, keep)
        if keep:
            chunks[i + 1][2][0] = done.pop()
    net_loss, sums = done

    total = pair_sum([sums] + [swapped(sums, "narrow", k) for k in range(1, n_narrow)])
    return (net_loss, total / P_SIZE)


def solution(mesh):
    return jax.shard_map(
        body,
        mesh=mesh,
        in_specs=(
            P("narrow"),
            P(("groups", "narrow")),
            P(("groups", "wide"), None, None, None),
            P(("groups", "wide"), None),
            P(("groups", "wide")),
            P(("groups", "wide")),
            P(("groups", "wide")),
            P(("groups", "wide"), None, None, None),
            P(("groups", "wide"), None),
        ),
        out_specs=(P("narrow", ("groups", "wide")), P(None, ("groups", "wide"))),
        check_vma=False,
    )
```

```python
import functools

import jax
import jax.numpy as jnp
from jax import lax
from jax.experimental import pallas as pl
from jax.experimental.pallas import tpu as pltpu
from jax.sharding import PartitionSpec as P

P_SIZE = 512
LANES = 128
ROWS = 16
DEST_CHUNK = 4
MXU = 256
CHUNKS = (80, 48)
VMEM_LIMIT = 63 << 20
NET_VMEM = 16 << 20

QUANTILE_MID = 2.6095163822174072
QUANTILE = (
    2.883376121520996,
    1.5978178977966309,
    0.023873422294855118,
    -0.0908193290233612,
    0.0662941262125969,
    -0.010339167900383472,
    -0.019267892464995384,
    0.011844170279800892,
    0.003007495542988181,
    -0.004063245374709368,
    -0.00016578214126639068,
    0.0005968576297163963,
)
CDF_SHIFT = 3.0
CDF_MID = 0.1666666716337204
CDF = (
    0.729083776473999,
    3.0559914112091064,
    8.280515670776367,
    10.208822250366211,
    -13.521076202392578,
    -54.16969680786133,
    43.550254821777344,
    285.4417419433594,
    -214.20135498046875,
    -1204.82958984375,
)
HALF_LOG2E = 0.7213475204444817


def horner(coefs, x):
    total = coefs[-1]
    for coef in coefs[-2::-1]:
        total = total * x + coef
    return total


def quantile(scaled):
    x = scaled.astype(jnp.float32) * (2.0**-31)
    s = 2.0 - jnp.log(1.0 - x * x)
    y = s * lax.rsqrt(s)
    return x * horner(QUANTILE, y - QUANTILE_MID)


def weighted_prob(t, exposure):
    y = jnp.abs(t)
    r = lax.rsqrt(y + CDF_SHIFT)
    q = r * r
    tail = jnp.exp2(t * t * -HALF_LOG2E) * q * horner(CDF, q - CDF_MID)
    return exposure * jnp.where(t > 0.0, 1.0 - tail, tail)


def fill_panel(panel, first, part, first_point):
    points = panel.shape[2]
    row = lax.broadcasted_iota(jnp.int32, (ROWS, LANES), 0) + first_point

    def fill(c, carry):
        at = pl.ds(pl.multiple_of(c * LANES, LANES), LANES)
        gen = part[0:1, at]
        shift = part[1:2, at]
        scaled = lax.shift_left(row * gen, 23) + (lax.shift_left(shift, 13) + (4096 - 2**31))
        jump = lax.shift_left(gen, 27)
        for r in range(points // ROWS):
            value = quantile(scaled).astype(jnp.bfloat16)
            rows = pl.ds(r * ROWS, ROWS)
            panel[0, first + c, rows, :] = value
            panel[1, first + c, rows, :] = pltpu.roll(value, LANES // 2, 1)
            scaled = scaled + jump
        return carry

    lax.fori_loop(0, part.shape[1] // LANES, fill, 0, unroll=part.shape[1] // LANES)


def panel_kernel(all_points, part, panel):
    fill_panel(panel, 0, part, lax.axis_index("narrow") * all_points)


def loss_kernel(n_parts, n_dest, split, direct, has_panel, all_points, first_point, pattern, *refs):
    me = lax.axis_index("narrow")
    base = lax.axis_index("wide") if direct else 0
    parts = refs[:n_parts]
    sources = refs[n_parts : n_parts + 4]
    outs = refs[n_parts + 4 : -8]
    panel, load_ref, thr_ref, expo_ref, seg_ref, even, odd, sems = refs[-8:]
    masked = (even, odd)
    points = panel.shape[2]
    blocks = load_ref.shape[0]
    columns = parts[-1].shape[1] // LANES
    seg_dev = (outs[0] if direct else outs[0].at[0]).shape[1]
    sub = seg_dev // (2 * MXU)
    group = split * sub
    steps = blocks // 2

    copies = [
        pltpu.make_async_copy(source, target, sems.at[i])
        for i, (source, target) in enumerate(zip(sources, (load_ref, thr_ref, expo_ref, seg_ref)))
    ]
    if has_panel:
        copies.append(
            pltpu.make_async_copy(parts[0], panel.at[:, pl.ds(me * columns, columns)], sems.at[4])
        )
    for copy in copies:
        copy.start()

    for k in range(int(has_panel), n_parts):
        fill_panel(panel, (me ^ k) * columns, parts[k], me * all_points + first_point)

    for copy in copies:
        copy.wait()

    low = lax.broadcasted_iota(jnp.int32, (points, LANES), 1) < LANES // 2
    seg_row = lax.broadcasted_iota(jnp.int32, (ROWS, LANES), 0)

    def picked(b):
        halves = []
        for k in (0, 2):
            q0 = pattern[k, b]
            q1 = pattern[k + 1, b]
            left = panel[q0 & 1, lax.shift_right_logical(q0, 1)]
            right = panel[1 - (q1 & 1), lax.shift_right_logical(q1, 1)]
            halves.append(jnp.where(low, left, right))
        return jnp.concatenate(halves, axis=1)

    def one_pass(chunk, sums, latents):
        def project(step, parity):
            b = 2 * step
            loads = jnp.concatenate([load_ref[b], load_ref[b + 1]], axis=1)
            pltpu.matmul_push_rhs(loads, parity, parity)
            pltpu.matmul_acc_lhs(
                latents[parity], jnp.concatenate([picked(b), picked(b + 1)], axis=0), parity
            )

        def push_onehot(step, parity):
            local = [seg_ref[pl.ds(2 * step + j, 1), :] & (2 * MXU - 1) for j in range(2)]
            low_rows = [jnp.where(seg_row == (at & (ROWS - 1)), 1.0, 0.0).astype(jnp.bfloat16) for at in local]
            high = [
                jnp.broadcast_to(lax.shift_right_logical(at, 4), (ROWS, LANES)).astype(jnp.int16)
                for at in local
            ]
            for n in range(2):
                tile = [
                    jnp.concatenate(
                        [
                            jnp.where(high[j] == jnp.int16(n * MXU // ROWS + r), low_rows[j], jnp.bfloat16(0))
                            for r in range(MXU // ROWS)
                        ],
                        axis=0,
                    )
                    for j in range(2)
                ]
                pltpu.matmul_push_rhs(jnp.concatenate(tile, axis=1), parity, n, transpose=True)

        def add_up(parity):
            for n in range(2):
                pltpu.matmul_acc_lhs(sums[n], masked[parity][...], parity)

        def weigh(step, parity, latent):
            for j in range(2):
                one = pl.ds(2 * step + j, 1)
                here = slice(j * LANES, (j + 1) * LANES)
                t = thr_ref[one, :] - latent[j * points : (j + 1) * points, here]
                prob = weighted_prob(t, expo_ref[one, :]).astype(jnp.bfloat16)
                part = lax.shift_right_logical(seg_ref[one, :], (2 * MXU).bit_length() - 1)
                part = (part ^ (base * sub)) - chunk * group
                part = jnp.broadcast_to(part, (ROWS, LANES)).astype(jnp.int16)
                for d in range(group):
                    mine = part == jnp.int16(d)
                    for r in range(0, points, ROWS):
                        masked[parity][d * points + r : d * points + r + ROWS, here] = jnp.where(
                            mine, prob[r : r + ROWS], jnp.bfloat16(0)
                        )

        def stage(step, parity, ahead=True, behind=True):
            latent = pltpu.matmul_pop(latents[parity])
            push_onehot(step, parity)
            if behind:
                add_up(1 - parity)
            if ahead:
                project(step + 1, 1 - parity)
            weigh(step, parity, latent)

        project(0, 0)
        stage(0, 0, behind=False)

        def pair(i, carry):
            stage(2 * i + 1, 1)
            stage(2 * i + 2, 0)
            return carry

        lax.fori_loop(0, steps // 2 - 1, pair, 0)
        stage(steps - 1, 1, ahead=False)
        add_up(1)

        for n in range(2):
            total = pltpu.matmul_pop(sums[n])
            for d in range(split):
                for i in range(sub):
                    at = slice(i * 2 * MXU + n * MXU, i * 2 * MXU + (n + 1) * MXU)
                    value = total[(d * sub + i) * points : (d * sub + i + 1) * points]
                    if direct:
                        outs[d][:, at] = value.astype(outs[d].dtype)
                    else:
                        outs[0][chunk * split + d, :, at] = value.astype(jnp.bfloat16)

    def passes(*accs):
        if n_dest == split:
            one_pass(0, accs[:2], accs[2:])
        else:
            lax.fori_loop(0, n_dest // split, lambda c, x: (one_pass(c, accs[:2], accs[2:]), x)[1], 0)

    pl.run_scoped(
        passes,
        *[pltpu.ACC(n)((group * points, MXU), jnp.float32) for n in range(2)],
        *[pltpu.ACC(n)((2 * points, MXU), jnp.float32) for n in range(2)],
    )


def net_kernel(first_point, n_received, has_before, pattern, tiles_ref, *refs):
    received = refs[:n_received]
    losses, net_rows, sem, keep_sem = refs[-4:]
    n_before = 2 if has_before else 0
    before = refs[n_received : n_received + n_before]
    keep = refs[n_received + n_before : -4]
    if len(keep) == 4:
        keep_in, out_ref, sums_ref, keep_out = keep
        keep_copy = pltpu.make_async_copy(keep_in, keep_out, keep_sem)
        keep_copy.start()
    else:
        keep_copy = None
        out_ref, sums_ref = keep
    blocks = tiles_ref.shape[0]
    points = losses.shape[1]
    slots = tiles_ref.shape[1] // LANES
    for q in range(blocks):
        at = slice(q * LANES, (q + 1) * LANES)
        if n_received == 1:
            total = jnp.sum(received[0][:, :, at].astype(jnp.float32), axis=0)
        else:
            total = received[0][:, at].astype(jnp.float32)
            for ref in received[1:]:
                total = total + ref[:, at].astype(jnp.float32)
        losses[q] = total.astype(jnp.bfloat16)
    for b in range(blocks):
        at = slice(b * LANES, (b + 1) * LANES)
        picked = jnp.concatenate([losses[pattern[b, k]] for k in range(slots)], axis=1)
        net = jnp.dot(picked, tiles_ref[b], preferred_element_type=jnp.float32)
        net_rows[:, at] = net
        first = jnp.sum(net, axis=0, keepdims=True)
        second = jnp.sum(net * net, axis=0, keepdims=True)
        if before:
            first += before[0][0:1, at]
            second += before[0][1:2, at]
        sums_ref[0:1, at] = first
        sums_ref[1:2, at] = second
    copy = pltpu.make_async_copy(net_rows, out_ref.at[pl.ds(first_point, points), :], sem)
    copy.start()
    copy.wait()
    if keep_copy is not None:
        keep_copy.wait()


def net_call(net_pattern, tiles, received, first_point, chunk, points, seg_dev, before, keep):
    vmem = pl.BlockSpec(memory_space=pltpu.VMEM)
    hbm = pl.BlockSpec(memory_space=pltpu.HBM)
    extra = [] if before is None else [before[1], before[0]]
    return pl.pallas_call(
        functools.partial(net_kernel, first_point, len(received), before is not None),
        out_shape=[
            jax.ShapeDtypeStruct((points, seg_dev), jnp.float32),
            jax.ShapeDtypeStruct((2, seg_dev), jnp.float32),
        ]
        + [jax.ShapeDtypeStruct(k.shape, k.dtype) for k in keep],
        in_specs=[pl.BlockSpec(memory_space=pltpu.SMEM)]
        + [vmem] * (1 + len(received))
        + [vmem, hbm][: len(extra)]
        + [hbm] * len(keep),
        out_specs=[hbm, vmem] + [vmem] * len(keep),
        scratch_shapes=[
            pltpu.VMEM((seg_dev // LANES, chunk, LANES), jnp.bfloat16),
            pltpu.VMEM((chunk, seg_dev), jnp.float32),
            pltpu.SemaphoreType.DMA,
            pltpu.SemaphoreType.DMA,
        ],
        input_output_aliases={} if before is None else {3 + len(received): 0},
        compiler_params=pltpu.CompilerParams(vmem_limit_bytes=NET_VMEM),
        name="net",
    )(net_pattern, tiles, *received, *extra, *keep)


def loss_call(pattern, parts, has_panel, loadings, threshold, exposure, segment_map, n_dest, all_points, first_point, points, seg_dev, direct):
    blocks = loadings.shape[0]
    n_parts = len(parts)
    columns = parts[-1].shape[1] // LANES * n_parts
    split = min(n_dest, DEST_CHUNK)
    if direct:
        out_shape = [
            jax.ShapeDtypeStruct((points, seg_dev), jnp.bfloat16 if d else jnp.float32)
            for d in range(n_dest)
        ]
    else:
        out_shape = [jax.ShapeDtypeStruct((n_dest, points, seg_dev), jnp.bfloat16)]
    slot = pltpu.VMEM((split * seg_dev // (2 * MXU) * points, MXU), jnp.bfloat16)
    vmem = pl.BlockSpec(memory_space=pltpu.VMEM)
    smem = pl.BlockSpec(memory_space=pltpu.SMEM)
    hbm = pl.BlockSpec(memory_space=pltpu.HBM)
    return pl.pallas_call(
        functools.partial(loss_kernel, n_parts, n_dest, split, direct, has_panel, all_points, first_point),
        out_shape=out_shape,
        in_specs=[smem, hbm if has_panel else vmem] + [vmem] * (n_parts - 1) + [hbm] * 4,
        out_specs=[vmem] * len(out_shape),
        scratch_shapes=[
            pltpu.VMEM((2, columns, points, LANES), jnp.bfloat16),
            pltpu.VMEM((blocks, 256, LANES), jnp.bfloat16),
            pltpu.VMEM((blocks, LANES), jnp.float32),
            pltpu.VMEM((blocks, LANES), jnp.float32),
            pltpu.VMEM((blocks, LANES), jnp.int32),
            slot,
            slot,
            pltpu.SemaphoreType.DMA((5,)),
        ],
        compiler_params=pltpu.CompilerParams(vmem_limit_bytes=VMEM_LIMIT),
        name="loss",
    )(
        pattern,
        *parts,
        loadings.reshape(blocks, 256, LANES),
        threshold.reshape(blocks, LANES),
        exposure.reshape(blocks, LANES),
        segment_map.reshape(blocks, LANES),
    )


def shifted(x, axis, k):
    n = lax.axis_size(axis)
    return lax.ppermute(x, axis, [(i, (i + k) % n) for i in range(n)])


def swapped(x, axis, k):
    return lax.ppermute(x, axis, [(i, i ^ k) for i in range(lax.axis_size(axis))])


def pair_sum(terms):
    while len(terms) > 1:
        terms = [terms[i] + terms[i + 1] for i in range(0, len(terms), 2)]
    return terms[0]


def body(
    generator,
    lattice_shift,
    loadings,
    load_pattern,
    threshold,
    exposure,
    segment_map,
    net_tiles,
    net_pattern,
):
    n_narrow = lax.axis_size("narrow")
    n_dest = lax.axis_size("wide")
    points = P_SIZE // n_narrow
    seg_blocks = net_tiles.shape[0]
    seg_dev = seg_blocks * LANES
    direct = n_dest <= 8

    own = jnp.stack([generator, lattice_shift])
    parts = [swapped(own, "narrow", k) for k in range(1, n_narrow)]
    vmem = pl.BlockSpec(memory_space=pltpu.VMEM)
    own_panel = pl.pallas_call(
        functools.partial(panel_kernel, points),
        out_shape=jax.ShapeDtypeStruct(
            (2, own.shape[1] // LANES, CHUNKS[0] * points // sum(CHUNKS), LANES), jnp.bfloat16
        ),
        in_specs=[vmem],
        out_specs=vmem,
        name="panel",
    )(own)
    pattern = load_pattern.T
    slots = net_tiles.shape[1]
    tiles = net_tiles.reshape(seg_blocks, slots * LANES, LANES)
    chunks = []
    first = 0
    for chunk in CHUNKS:
        chunk = chunk * points // sum(CHUNKS)
        partial = loss_call(
            pattern,
            [own_panel if first == 0 else own] + parts,
            first == 0,
            loadings,
            threshold,
            exposure,
            segment_map,
            n_dest,
            points,
            first,
            chunk,
            seg_dev,
            direct,
        )
        if direct:
            received = [partial[0]] + [swapped(partial[k], "wide", k) for k in [*range(2, n_dest), *range(1, min(2, n_dest))]]
        else:
            received = [lax.all_to_all(partial[0], "wide", split_axis=0, concat_axis=0, tiled=True)]
        chunks.append((first, chunk, received))
        first += chunk
    done = None
    for i, (first, chunk, received) in enumerate(chunks):
        keep = [chunks[i + 1][2][0]] if direct and i + 1 < len(chunks) else []
        *done, = net_call(net_pattern, tiles, received, first, chunk, points, seg_dev, done, keep)
        if keep:
            chunks[i + 1][2][0] = done.pop()
    net_loss, sums = done

    total = pair_sum([sums] + [swapped(sums, "narrow", k) for k in range(1, n_narrow)])
    return (net_loss, total / P_SIZE)


def solution(mesh):
    return jax.shard_map(
        body,
        mesh=mesh,
        in_specs=(
            P("narrow"),
            P(("groups", "narrow")),
            P(("groups", "wide"), None, None, None),
            P(("groups", "wide"), None),
            P(("groups", "wide")),
            P(("groups", "wide")),
            P(("groups", "wide")),
            P(("groups", "wide"), None, None, None),
            P(("groups", "wide"), None),
        ),
        out_specs=(P("narrow", ("groups", "wide")), P(None, ("groups", "wide"))),
        check_vma=False,
    )
```
